256 devices in a mesh: tower: 16 (over z, x_hi), plate: 16 (over y, x_lo, core).
Axes of the slice: x: 4 (x_hi: 2, x_lo: 2; x = x_hi * 2 + x_lo), y: 4, z: 8, core: 2. Of those that a mesh axis runs over, the one named last changes fastest.
Arguments:
- features: bfloat16 [16, 4096, 128], P('tower', 'plate'), may hold values from -6 to 6
- adjoint: bfloat16 [16, 4096, 128], P('tower', 'plate'), may hold values from -6 to 6
- positions: bfloat16 [3, 16, 4096], P(None, 'tower', 'plate'), may hold values from 0 to 1
- w_rbf: bfloat16 [16, 128], replicated, may hold values from -1.5 to 1.5
- b_rbf: float32 [128], replicated, may hold values from -1 to 1
- w_filter: bfloat16 [128, 128], replicated, may hold values from -0.5 to 0.5
- b_filter: float32 [128], replicated, may hold values from -1 to 1
- atom_counts: int32 [16, 16], P('tower', 'plate'), may hold values from 128 to 256, as said below
- tile_counts: int32 [16, 16], P('tower', 'plate'), may hold values from 1 to 56, as said below
- tower_tiles: int32 [16, 16, 56], P('tower', 'plate'), may hold values from 0 to 23
- plate_tiles: int32 [16, 16, 56], P('tower', 'plate'), may hold values from 0 to 127
- image_shifts: int32 [16, 16, 56], P('tower', 'plate'), may hold values from 0 to 8
Outputs:
- grad_features: float32 [16, 4096, 128], P('tower', 'plate')
- grad_positions: float32 [3, 16, 4096], P(None, 'tower', 'plate')
- grad_w_rbf: float32 [16, 128], replicated
- grad_b_rbf: float32 [128], replicated
- grad_w_filter: float32 [128, 128], replicated
- grad_b_filter: float32 [128], replicated
The draws below stay inside these ranges and needn't reach their ends.
Inputs may be any that keep to these rules, and one draw needn't show every extreme that they name: `atom_counts`: 256 in at least one brick. `tile_counts`: 56 in at least one brick; entries past the count are unused. `tower_tiles`: tiles below 8 lie in the brick below, the next 8 in the brick itself, the rest in the brick above. `plate_tiles`: tile v lies in brick v // 8 of the same plate. `image_shifts`: shift c moves the receiver by c // 3 - 1 along x and c % 3 - 1 along y.
All inputs are finite; a program needn't handle non-finite values.
Results may differ from the reference program's by a relative error of at most 0.005.
Values may be sent and summed in bfloat16 or wider, within the bound.
A program may use at most 64 MiB of HBM per device.

```python
import math
import jax
import jax.numpy as jnp
from jax import lax

F = 128
NRBF = 16
ATOMS = 256
TILE = 32
MAXT = 56
TOWER_TILES = 24
BRICKS_Z = 16
BRICKS_XY = 16
PLATE_TILES = 128


def draw_atom_counts(key, part):
    key_one, key_two = jax.random.split(jax.random.fold_in(key, 11))
    bricks = BRICKS_Z * BRICKS_XY
    counts = jax.random.randint(key_one, (bricks,), ATOMS // 2, ATOMS + 1)
    chosen = jax.random.randint(key_two, (), 0, bricks)
    counts = jnp.where(jnp.arange(bricks) == chosen, ATOMS, counts)
    return counts.reshape(BRICKS_Z, BRICKS_XY).astype(jnp.int32)


def draw_tile_counts(key, part):
    key_one, key_two = jax.random.split(jax.random.fold_in(key, 23))
    bricks = BRICKS_Z * BRICKS_XY
    divisor = jax.random.randint(key_one, (bricks,), 1, 5)
    counts = jnp.maximum(1, MAXT // divisor)
    chosen = jax.random.randint(key_two, (), 0, bricks)
    counts = jnp.where(jnp.arange(bricks) == chosen, MAXT, counts)
    return counts.reshape(BRICKS_Z, BRICKS_XY).astype(jnp.int32)


def place_ends(drawn, own_key, smallest, largest):
    extent = drawn.shape
    index_at = [jax.random.randint(jax.random.fold_in(own_key, axis), (), 0, extent[axis]) for axis in range(len(extent))]
    drawn = drawn.at[tuple(index_at)].set(smallest)
    longest = extent.index(max(extent))
    index_at[longest] = (index_at[longest] + 1) % extent[longest]
    return drawn.at[tuple(index_at)].set(largest)


def steps_of(key, extent, shards, least, top_value):
    def one(position, parts):
        heights = jax.random.uniform(jax.random.fold_in(jax.random.fold_in(key, 6), position), (parts,), jnp.float32, least / len(shards), top_value / len(shards))
        return jnp.repeat(jnp.exp(heights), extent[position] // parts).reshape((-1,) + (1,) * (len(extent) - position - 1))

    loudness = one(*shards[0])
    for cut in shards[1:]:
        loudness = loudness * one(*cut)
    return loudness


def centred(key, shape, width, bound, shards=(), kind=jnp.bfloat16):
    entries = jax.random.normal(key, shape, jnp.float32) * width
    if len(shards) > 0:
        entries = steps_of(key, shape, shards, -0.22, 0.18) * entries
    return jnp.clip(entries, min=-bound, max=bound).astype(kind)


def setup_inputs(seed: int = 0) -> dict:
    keys = jax.random.split(jax.random.key(seed), 13)
    return {
        "features": centred(keys[0], (BRICKS_Z, BRICKS_XY * ATOMS, F), 1.0, 6.0, ((0, 16), (1, 16))),
        "adjoint": centred(keys[1], (BRICKS_Z, BRICKS_XY * ATOMS, F), 1.0, 6.0, ((0, 16), (1, 16))),
        "positions": jnp.clip(1.0 * jax.random.uniform(keys[2], (3, BRICKS_Z, BRICKS_XY * ATOMS), jnp.float32) ** steps_of(keys[2], (3, BRICKS_Z, BRICKS_XY * ATOMS), ((1, 16), (2, 16)), -0.2, 0.2), 0.0, 1.0).astype(jnp.bfloat16),
        "w_rbf": centred(keys[3], (NRBF, F), NRBF ** -0.5, 1.5),
        "b_rbf": jnp.clip(jax.random.uniform(keys[4], (F,), jnp.float32, -1.0, 1.0), -1.0, 1.0),
        "w_filter": centred(keys[5], (F, F), F ** -0.5, 0.5),
        "b_filter": jnp.clip(jax.random.uniform(keys[6], (F,), jnp.float32, -1.0, 1.0), -1.0, 1.0),
        "atom_counts": draw_atom_counts(jax.random.fold_in(keys[12], 71), 0),
        "tile_counts": draw_tile_counts(jax.random.fold_in(keys[12], 71), 0),
        "tower_tiles": place_ends(jax.random.randint(keys[9], (BRICKS_Z, BRICKS_XY, MAXT), 0, TOWER_TILES), jax.random.fold_in(keys[9], 1), 0, TOWER_TILES - 1).astype(jnp.int32),
        "plate_tiles": place_ends(jax.random.randint(keys[10], (BRICKS_Z, BRICKS_XY, MAXT), 0, PLATE_TILES), jax.random.fold_in(keys[10], 1), 0, PLATE_TILES - 1).astype(jnp.int32),
        "image_shifts": place_ends(jax.random.randint(keys[11], (BRICKS_Z, BRICKS_XY, MAXT), 0, 9), jax.random.fold_in(keys[11], 1), 0, 8).astype(jnp.int32),
    }


box_side = 1.0
brick_height = 1.0
cutoff_radius = 3.0
soften = 0.01
sharpness = 10.0
log_two = math.log(2.0)

def shift_vector(shift_code, tower_tile, per_brick):
    step_z = tower_tile // per_brick - 1
    return jnp.stack([(shift_code // 3 - 1).astype(jnp.float32) * box_side, (shift_code % 3 - 1).astype(jnp.float32) * box_side, step_z.astype(jnp.float32) * brick_height])

def pair_tile(adj_rows, recv_pos, feat_rows, send_pos, shift_vec, w_rbf, b_rbf, w_filter, b_filter):
    size_recv = adj_rows.shape[0]
    size_send = feat_rows.shape[0]
    feat_width = adj_rows.shape[1]
    displace = recv_pos[:, :, None] + shift_vec[:, None, None] - send_pos[:, None, :]
    distance = jnp.sqrt(lax.optimization_barrier(jnp.sum(displace * displace, axis=0)) + soften).reshape(-1)
    nbasis = w_rbf.shape[0]
    centres = jnp.arange(nbasis, dtype=jnp.float32) * (cutoff_radius / (nbasis - 1))
    offsets = distance[None, :] - centres[:, None]
    basis = jnp.exp(-sharpness * offsets * offsets)
    basis_b = basis.astype(jnp.bfloat16)
    preact = lax.dot_general(basis_b, w_rbf, (((0,), (0,)), ((), ())), preferred_element_type=jnp.float32) + b_rbf
    softed = (jax.nn.softplus(preact) - log_two).astype(jnp.bfloat16)
    filter_raw = jnp.dot(softed, w_filter, preferred_element_type=jnp.float32) + b_filter
    inside = distance < cutoff_radius
    phase_arg = math.pi / cutoff_radius * distance
    envelope = jnp.where(inside, 0.5 * (jnp.cos(phase_arg) + 1.0), 0.0)
    slope = jnp.where(inside, -0.5 * (math.pi / cutoff_radius) * jnp.sin(phase_arg), 0.0)
    adj_wide = adj_rows.astype(jnp.float32)
    feat_wide = feat_rows.astype(jnp.float32)
    filtered = (filter_raw * envelope[:, None]).reshape(size_recv, size_send, feat_width)
    grad_rows = jnp.einsum('if,ijf->jf', adj_wide, filtered)
    adjoint_pair = (adj_wide[:, None, :] * feat_wide[None, :, :]).reshape(size_recv * size_send, feat_width)
    d_raw = adjoint_pair * envelope[:, None]
    d_raw_b = d_raw.astype(jnp.bfloat16)
    grad_bf = lax.optimization_barrier(jnp.sum(d_raw, axis=0))
    grad_wf = lax.dot_general(softed, d_raw_b, (((0,), (0,)), ((), ())), preferred_element_type=jnp.float32)
    d_soft = lax.dot_general(d_raw_b, w_filter, (((1,), (1,)), ((), ())), preferred_element_type=jnp.float32)
    d_pre = d_soft * jax.nn.sigmoid(preact)
    d_pre_b = d_pre.astype(jnp.bfloat16)
    grad_br = lax.optimization_barrier(jnp.sum(d_pre, axis=0))
    grad_wr = lax.dot_general(basis_b, d_pre_b, (((1,), (0,)), ((), ())), preferred_element_type=jnp.float32)
    d_basis = lax.dot_general(w_rbf, d_pre_b, (((1,), (1,)), ((), ())), preferred_element_type=jnp.float32)
    d_dist = lax.optimization_barrier(jnp.sum(d_basis * basis * (-2.0 * sharpness) * offsets, axis=0))
    d_dist = d_dist + lax.optimization_barrier(jnp.sum(adjoint_pair * filter_raw, axis=1)) * slope
    radial = (d_dist / distance).reshape(size_recv, size_send)
    pull = displace * radial[None]
    return (grad_rows, lax.optimization_barrier(jnp.sum(pull, axis=2)), -lax.optimization_barrier(jnp.sum(pull, axis=1)), (grad_wr, grad_br, grad_wf, grad_bf))

def add_into(array, piece, starts):
    current = lax.dynamic_slice(array, starts, piece.shape)
    return lax.dynamic_update_slice(array, current + piece, starts)

def reference(features, adjoint, positions, w_rbf, b_rbf, w_filter, b_filter, atom_counts, tile_counts, tower_tiles, plate_tiles, image_shifts):
    tower_count = BRICKS_Z
    plate_count = BRICKS_XY
    per_brick = ATOMS // TILE
    feat_width = features.shape[2]
    slots = jnp.arange(ATOMS, dtype=jnp.int32)
    live_mask = (slots[None, None, :] < atom_counts[:, :, None]).reshape(tower_count, plate_count * ATOMS)
    zero_b = jnp.zeros((), jnp.bfloat16)
    feat_live = jnp.where(live_mask[:, :, None], features, zero_b)
    adj_live = jnp.where(live_mask[:, :, None], adjoint, zero_b)
    coords = positions.astype(jnp.float32)
    initial = (jnp.zeros(features.shape, jnp.float32), jnp.zeros(coords.shape, jnp.float32), (jnp.zeros(w_rbf.shape, jnp.float32), jnp.zeros(b_rbf.shape, jnp.float32), jnp.zeros(w_filter.shape, jnp.float32), jnp.zeros(b_filter.shape, jnp.float32)))

    def visit(index, totals):
        brick = index // MAXT
        entry = index % MAXT
        tower_i = (brick // plate_count).astype(jnp.int32)
        plate_i = (brick % plate_count).astype(jnp.int32)

        def work(totals):
            acc_dh, acc_gp, acc_weights = totals
            tower_tile = tower_tiles[tower_i, plate_i, entry]
            plate_tile = plate_tiles[tower_i, plate_i, entry]
            shift_code = image_shifts[tower_i, plate_i, entry]
            source_z = ((tower_i + tower_tile // per_brick - 1) % tower_count).astype(jnp.int32)
            recv_start = (plate_i * ATOMS + tower_tile % per_brick * TILE).astype(jnp.int32)
            send_start = (plate_tile * TILE).astype(jnp.int32)
            adj_rows = lax.dynamic_slice(adj_live, (source_z, recv_start, jnp.int32(0)), (1, TILE, feat_width))[0]
            recv_pos = lax.dynamic_slice(coords, (jnp.int32(0), source_z, recv_start), (3, 1, TILE))[:, 0]
            feat_rows = lax.dynamic_slice(feat_live, (tower_i, send_start, jnp.int32(0)), (1, TILE, feat_width))[0]
            send_pos = lax.dynamic_slice(coords, (jnp.int32(0), tower_i, send_start), (3, 1, TILE))[:, 0]
            shift_vec = shift_vector(shift_code, tower_tile, per_brick)
            grad_rows, grad_recv, grad_send, grad_weights = pair_tile(adj_rows, recv_pos, feat_rows, send_pos, shift_vec, w_rbf, b_rbf, w_filter, b_filter)
            acc_dh = add_into(acc_dh, grad_rows[None], (tower_i, send_start, jnp.int32(0)))
            acc_gp = add_into(acc_gp, grad_send[:, None, :], (jnp.int32(0), tower_i, send_start))
            acc_gp = add_into(acc_gp, grad_recv[:, None, :], (jnp.int32(0), source_z, recv_start))
            acc_weights = jax.tree.map(lambda left, right: left + right, acc_weights, grad_weights)
            return (acc_dh, acc_gp, acc_weights)
        return lax.cond(entry < tile_counts[tower_i, plate_i], work, lambda kept: kept, totals)
    acc_dh, acc_gp, acc_weights = lax.fori_loop(0, tower_count * plate_count * MAXT, visit, initial)
    total_tiles = jnp.sum(tile_counts).astype(jnp.float32)
    scale = 1.0 / jnp.sqrt(total_tiles * (TILE * TILE))
    grad_features = jnp.where(live_mask[:, :, None], acc_dh, 0.0)
    return (grad_features, acc_gp, acc_weights[0] * scale, acc_weights[1] * scale, acc_weights[2] * scale, acc_weights[3] * scale)
```

```python
import math

import jax
import jax.numpy as jnp
from jax import lax
from jax.experimental import pallas as pl
from jax.experimental.pallas import tpu as pltpu

F = 128
TILE = 32
PAIRS = TILE * TILE
MAXT = 56
ROWS = 64
TOWER = 24
PLATE = 128
NRBF = 16
cutoff = 3.0
soften = 0.01
sharp = 10.0
f32 = jnp.float32
bf16 = jnp.bfloat16

NN = (((1,), (0,)), ((), ()))
NT = (((1,), (1,)), ((), ()))
TN = (((0,), (0,)), ((), ()))


def dot(a, b, dims=NN):
    return lax.dot_general(a, b, dims, preferred_element_type=f32)


def iota(shape, axis):
    return lax.broadcasted_iota(jnp.int32, shape, axis)


def split(x):
    hi = x.astype(bf16)
    return hi, (x - hi.astype(f32)).astype(bf16)


def pairs_kernel(
    cnt_s, u_s, v_s,
    adj_ref, feat_ref, tpos_ref, ppos_ref, col_ref, row_ref,
    w1_ref, wr_ref, nwft_ref, hwf_ref,
    gf_ref, gs_ref, gr_ref, gw_ref,
    disp_ref, dist_ref, env_ref, tan_ref, dd_ref, rep_ref,
    *, chunk,
):
    count = cnt_s[0]
    rep = (iota((TILE, PAIRS), 1) // TILE == iota((TILE, PAIRS), 0)).astype(bf16)
    til = (iota((TILE, PAIRS), 1) % TILE == iota((TILE, PAIRS), 0)).astype(bf16)
    rep_ref[...] = rep
    ucol = col_ref[:, 0:1]
    vcol = col_ref[:, 1:2]
    ccol = col_ref[:, 2:3]
    pick_u = (ucol == iota((ROWS, TOWER), 1)).astype(bf16)
    pick_v = (vcol == iota((ROWS, PLATE), 1)).astype(bf16)
    shifts = (ccol // 3 - 1, ccol % 3 - 1, ucol // 8 - 1)
    square = jnp.zeros((ROWS, PAIRS), f32)
    for d in range(3):
        recv = dot(pick_u, tpos_ref[d]).astype(bf16)
        send = dot(pick_v, ppos_ref[d]).astype(bf16)
        disp = dot(recv, rep) - dot(send, til) + shifts[d].astype(f32)
        disp_ref[d] = disp
        square = square + disp * disp
    dist = jnp.sqrt(square + soften)
    dist_ref[...] = dist
    theta = dist * (math.pi / (2 * cutoff))
    inside = (dist < cutoff) & (iota((ROWS, PAIRS), 0) < count)
    cosine = jnp.maximum(jnp.cos(theta), 1e-6)
    env_ref[...] = jnp.where(inside, cosine * cosine, 0.0)
    tan_ref[...] = jnp.where(inside, (-math.pi / cutoff) * jnp.sin(theta) / cosine, 0.0)
    dd_ref[...] = jnp.zeros((ROWS, PAIRS), f32)
    gf_ref[...] = jnp.zeros(gf_ref.shape, f32)
    gw_ref[...] = jnp.zeros(gw_ref.shape, f32)

    centres = iota((NRBF, 1), 0).astype(f32) * (cutoff / (NRBF - 1))
    ones = jnp.ones((NRBF, chunk), bf16)
    w1 = w1_ref[...]
    wr = wr_ref[...]
    nwft = nwft_ref[...]
    hwf = hwf_ref[...]
    fold = (iota((TILE, F), 1) % TILE == iota((TILE, F), 0)).astype(bf16)
    one_row = jnp.ones((NRBF, F), bf16)

    def body(e, carry):
        u = u_s[e]
        v = v_s[e]
        adj = jnp.concatenate([adj_ref[u]] * 2, axis=0)
        feat = feat_ref[v].astype(f32)
        feat4 = jnp.concatenate([feat] * 4, axis=0).T
        wide = jnp.concatenate([feat4] * (chunk // F), axis=1)
        acc = jnp.zeros((F, F), f32)
        gw1 = jnp.zeros((F + NRBF, F), f32)
        gw2 = jnp.zeros((2 * NRBF, F), f32)
        for s in range(0, PAIRS, chunk):
            lanes = pl.ds(s, chunk)
            dist_r = dist_ref[pl.ds(e, 1), lanes]
            env_r = env_ref[pl.ds(e, 1), lanes]
            off = dist_r - centres
            basis = jnp.exp(-sharp * off * off)
            inputs = jnp.concatenate([basis.astype(bf16), ones], axis=0)
            half = dot(w1, inputs)
            t = jnp.tanh(half)
            soft_b = jnp.concatenate([jnp.log(1.0 - t).astype(bf16), ones], axis=0)
            env_hi, env_lo = split(env_r)
            member = rep_ref[:, lanes]
            spread = jnp.concatenate([member * env_hi, member * env_lo], axis=0)
            adj_env = dot(adj, spread, TN)
            d_raw_b = (adj_env * wide).astype(bf16)
            filt = dot(nwft, soft_b)
            d_soft = dot(hwf, d_raw_b)
            d_pre_b = (d_soft * (1.0 + t)).astype(bf16)
            y = adj_env * filt
            for q in range(0, chunk, F):
                acc = acc + y[:, q:q + F]
            z_b = (y * wide).astype(bf16)
            zsum = dot(one_row, z_b)[0:1]
            d_basis = dot(wr, d_pre_b)
            d_dist = jnp.sum(d_basis * basis * off, axis=0, keepdims=True) * (-2.0 * sharp)
            dd_ref[pl.ds(e, 1), lanes] = d_dist + tan_ref[pl.ds(e, 1), lanes] * zsum
            gw1 = gw1 + dot(soft_b, d_raw_b, NT)
            gw2 = gw2 + dot(inputs, d_pre_b, NT)
        gf_ref[v] += dot(fold, acc.astype(bf16), NT)
        gw_ref[0:F + NRBF] += gw1
        gw_ref[F + NRBF:F + 3 * NRBF] += gw2
        return carry

    lax.fori_loop(0, count, body, 0)

    radial = dd_ref[...] / dist_ref[...]
    put_u = (row_ref[0:1] == iota((TOWER, ROWS), 0)).astype(bf16)
    put_v = (row_ref[1:2] == iota((PLATE, ROWS), 0)).astype(bf16)
    for d in range(3):
        hi, lo = split(disp_ref[d] * radial)
        recv_hi, recv_lo = split(dot(hi, rep, NT) + dot(lo, rep, NT))
        send_hi, send_lo = split(dot(hi, til, NT) + dot(lo, til, NT))
        gr_ref[d] = dot(put_u, recv_hi) + dot(put_u, recv_lo)
        gs_ref[d] = -(dot(put_v, send_hi) + dot(put_v, send_lo))


def parts_of(x):
    hi = x.astype(bf16)
    rest = x - hi.astype(f32)
    mid = rest.astype(bf16)
    low = (rest - mid.astype(f32)).astype(bf16)
    return [hi, mid, low]


def pairs(count, tower_tiles, plate_tiles, shifts, adj, feat, tpos, ppos, w_rbf, b_rbf, w_filter, b_filter, chunk=256):
    padded = jnp.pad(jnp.stack([tower_tiles, plate_tiles, shifts]), ((0, 0), (0, ROWS - MAXT)))
    zeros = [jnp.zeros((F,), bf16)] * (NRBF - 3)
    w1 = jnp.concatenate([(w_rbf * 0.5).T, jnp.stack(parts_of(b_rbf * 0.5) + zeros, axis=1)], axis=1)
    nwft = jnp.concatenate([-w_filter.T, jnp.stack(parts_of(b_filter) + zeros, axis=1)], axis=1)
    smem = pl.BlockSpec(memory_space=pltpu.SMEM)
    vmem = pl.BlockSpec(memory_space=pltpu.VMEM)
    return pl.pallas_call(
        lambda *refs: pairs_kernel(*refs, chunk=chunk),
        out_shape=(
            jax.ShapeDtypeStruct((PLATE, TILE, F), f32),
            jax.ShapeDtypeStruct((3, PLATE, TILE), f32),
            jax.ShapeDtypeStruct((3, TOWER, TILE), f32),
            jax.ShapeDtypeStruct((F + 3 * NRBF, F), f32),
        ),
        in_specs=[smem] * 3 + [vmem] * 10,
        out_specs=[vmem] * 4,
        scratch_shapes=[
            pltpu.VMEM((3, ROWS, PAIRS), f32),
            pltpu.VMEM((ROWS, PAIRS), f32),
            pltpu.VMEM((ROWS, PAIRS), f32),
            pltpu.VMEM((ROWS, PAIRS), f32),
            pltpu.VMEM((ROWS, PAIRS), f32),
            pltpu.VMEM((TILE, PAIRS), bf16),
        ],
        compiler_params=pltpu.CompilerParams(vmem_limit_bytes=40 << 20),
        name="pairs",
    )(count, tower_tiles, plate_tiles, adj, feat, tpos, ppos, padded.T, padded, w1, w_rbf, nwft, w_filter * jnp.asarray(0.5, bf16))


def shifted(block, axis, distance):
    devices = range(lax.axis_size(axis))
    route = [((i - distance) % len(devices), i) for i in devices]
    return lax.ppermute(block, axis, route)


def local(features, adjoint, positions, w_rbf, b_rbf, w_filter, b_filter, atom_counts, tile_counts, tower_tiles, plate_tiles, image_shifts):
    atoms = features.shape[1]
    live = jnp.arange(atoms, dtype=jnp.int32) < atom_counts[0, 0]
    zero = jnp.zeros((), bf16)
    own_feat = jnp.where(live[:, None], features[0], zero)
    own_adj = jnp.where(live[:, None], adjoint[0], zero)
    own_pos = positions[:, 0, :]
    below = shifted((own_adj, own_pos), "tower", 1)
    above = shifted((own_adj, own_pos), "tower", -1)
    tower_adj = jnp.concatenate([below[0], own_adj, above[0]], axis=0).reshape(TOWER, TILE, F)
    tower_pos = jnp.concatenate([below[1], own_pos, above[1]], axis=1).reshape(3, TOWER, TILE)
    plate_feat = lax.all_gather(own_feat, "plate", axis=0, tiled=True).reshape(PLATE, TILE, F)
    plate_pos = lax.all_gather(own_pos, "plate", axis=1, tiled=True).reshape(3, PLATE, TILE)
    gf, gs, gr, gw = pairs(
        tile_counts[0], tower_tiles[0, 0], plate_tiles[0, 0], image_shifts[0, 0],
        tower_adj, plate_feat, tower_pos, plate_pos, w_rbf, b_rbf, w_filter, b_filter,
    )
    home = lax.psum_scatter(gf.reshape(16, atoms, F), "plate", scatter_dimension=0, tiled=True)[0]
    home_pos = lax.psum_scatter(gs.reshape(3, 16, atoms), "plate", scatter_dimension=1, tiled=True)[:, 0]
    gr = gr.reshape(3, 3 * atoms)
    back_down = shifted(gr[:, :atoms], "tower", -1)
    back_up = shifted(gr[:, 2 * atoms:], "tower", 1)
    total_pos = home_pos + gr[:, atoms:2 * atoms] + back_down + back_up
    summed, tiles = lax.psum((gw, tile_counts[0, 0].astype(f32)), ("tower", "plate"))
    scale = lax.rsqrt(tiles * (TILE * TILE))
    return (
        jnp.where(live[:, None], home, 0.0)[None],
        total_pos[:, None, :],
        summed[F + NRBF:F + 2 * NRBF] * scale,
        summed[F + 2 * NRBF] * scale,
        summed[0:F] * -scale,
        summed[F] * scale,
    )


def solution(mesh):
    from jax.sharding import PartitionSpec as P
    brick = P("tower", "plate", None)
    one = P("tower", "plate")
    return jax.shard_map(
        local, mesh=mesh,
        in_specs=(brick, brick, P(None, "tower", "plate"), P(), P(), P(), P(), one, one, brick, brick, brick),
        out_specs=(brick, P(None, "tower", "plate"), P(), P(), P(), P()),
        check_vma=False,
    )
```

```python
import math

import jax
import jax.numpy as jnp
from jax import lax
from jax.experimental import pallas as pl
from jax.experimental.pallas import tpu as pltpu

F = 128
TILE = 32
PAIRS = TILE * TILE
MAXT = 56
ATOMS = 256
PACK = ATOMS + 32
BRICKS = 16
WROWS = 16
ROWS = 64
TOWER = 24
PLATE = 128
NRBF = 16
cutoff = 3.0
soften = 0.01
sharp = 10.0
f32 = jnp.float32
bf16 = jnp.bfloat16

NN = (((1,), (0,)), ((), ()))
NT = (((1,), (1,)), ((), ()))
TN = (((0,), (0,)), ((), ()))


def dot(a, b, dims=NN):
    return lax.dot_general(a, b, dims, preferred_element_type=f32)


def iota(shape, axis):
    return lax.broadcasted_iota(jnp.int32, shape, axis)


def split(x):
    hi = x.astype(bf16)
    return hi, (x - hi.astype(f32)).astype(bf16)


def pairs_kernel(
    cnt_s, u_s, v_s,
    tower_ref, plate_ref, col_ref, row_ref,
    w1_ref, wr_ref, nwft_ref, hwf_ref,
    pack_ref, tg_ref, gw_ref,
    disp_ref, dist_ref, env_ref, tan_ref, dd_ref, rep_ref, gf_ref,
    *, chunk,
):
    count = cnt_s[0]
    rep = (iota((TILE, PAIRS), 1) // TILE == iota((TILE, PAIRS), 0)).astype(bf16)
    rep_ref[...] = rep
    rep4 = (iota((F, PAIRS), 1) // TILE == iota((F, PAIRS), 0) % TILE).astype(bf16)
    til4 = (iota((F, PAIRS), 1) % TILE == iota((F, PAIRS), 0) % TILE).astype(bf16)
    ucol = col_ref[:, 0:1]
    vcol = col_ref[:, 1:2]
    ccol = col_ref[:, 2:3]
    group = iota((ROWS, F), 1) // TILE
    in_low_u, in_up_u = group == ucol % 8, group + 4 == ucol % 8
    in_low_v, in_up_v = group == vcol % 8, group + 4 == vcol % 8
    t_low = tower_ref[:, ATOMS:ATOMS + 16, :].reshape(48, F)
    t_up = tower_ref[:, ATOMS + 16:ATOMS + 32, :].reshape(48, F)
    p_low = plate_ref[:, ATOMS:ATOMS + 16, :].reshape(256, F)
    p_up = plate_ref[:, ATOMS + 16:ATOMS + 32, :].reshape(256, F)
    shifts = (ccol // 3 - 1, ccol % 3 - 1, ucol // 8 - 1)
    square = jnp.zeros((ROWS, PAIRS), f32)
    for d in range(3):
        pick_u = (ucol // 8 * 16 + d == iota((ROWS, 48), 1)).astype(bf16)
        pick_v = (vcol // 8 * 16 + d == iota((ROWS, 256), 1)).astype(bf16)
        recv = jnp.where(in_low_u, dot(pick_u, t_low), 0.0) + jnp.where(in_up_u, dot(pick_u, t_up), 0.0)
        send = jnp.where(in_low_v, dot(pick_v, p_low), 0.0) + jnp.where(in_up_v, dot(pick_v, p_up), 0.0)
        disp = dot(recv.astype(bf16), rep4) - dot(send.astype(bf16), til4) + shifts[d].astype(f32)
        disp_ref[d] = disp
        square = square + disp * disp
    dist = jnp.sqrt(square + soften)
    dist_ref[...] = dist
    theta = dist * (math.pi / (2 * cutoff))
    inside = (dist < cutoff) & (iota((ROWS, PAIRS), 0) < count)
    cosine = jnp.maximum(jnp.cos(theta), 1e-6)
    env_ref[...] = jnp.where(inside, cosine * cosine, 0.0)
    tan_ref[...] = jnp.where(inside, (-math.pi / cutoff) * jnp.sin(theta) / cosine, 0.0)
    dd_ref[...] = jnp.zeros((ROWS, PAIRS), f32)
    gf_ref[...] = jnp.zeros(gf_ref.shape, f32)
    gw_ref[...] = jnp.zeros(gw_ref.shape, f32)

    centres = iota((NRBF, 1), 0).astype(f32) * (cutoff / (NRBF - 1))
    ones = jnp.ones((NRBF, chunk), bf16)
    w1 = w1_ref[...]
    wr = wr_ref[...]
    nwft = nwft_ref[...]
    hwf = hwf_ref[...]
    fold = (iota((TILE, 2 * F), 1) % TILE == iota((TILE, 2 * F), 0)).astype(bf16)
    one_row = jnp.ones((NRBF, F), bf16)

    def body(e, carry):
        u = u_s[e]
        v = v_s[e]
        adj = tower_ref[u // 8, pl.ds(pl.multiple_of(u % 8 * TILE, TILE), TILE), :]
        adj = jnp.concatenate([adj] * 2, axis=0)
        feat = plate_ref[v // 8, pl.ds(pl.multiple_of(v % 8 * TILE, TILE), TILE), :].astype(f32)
        feat4 = jnp.concatenate([feat] * 4, axis=0).T
        wide = jnp.concatenate([feat4] * (chunk // F), axis=1)
        acc = jnp.zeros((F, F), f32)
        gw1 = jnp.zeros((F + NRBF, F), f32)
        gw2 = jnp.zeros((2 * NRBF, F), f32)
        for s in range(0, PAIRS, chunk):
            lanes = pl.ds(s, chunk)
            dist_r = dist_ref[pl.ds(e, 1), lanes]
            env_r = env_ref[pl.ds(e, 1), lanes]
            off = dist_r - centres
            basis = jnp.exp(-sharp * off * off)
            inputs = jnp.concatenate([basis.astype(bf16), ones], axis=0)
            half = dot(w1, inputs)
            t = jnp.tanh(half)
            soft_b = jnp.concatenate([jnp.log(1.0 - t).astype(bf16), ones], axis=0)
            env_hi, env_lo = split(env_r)
            member = rep_ref[:, lanes]
            spread = jnp.concatenate([member * env_hi, member * env_lo], axis=0)
            adj_env = dot(adj, spread, TN)
            d_raw_b = (adj_env * wide).astype(bf16)
            filt = dot(nwft, soft_b)
            d_soft = dot(hwf, d_raw_b)
            d_pre_b = (d_soft * (1.0 + t)).astype(bf16)
            y = adj_env * filt
            for q in range(0, chunk, F):
                acc = acc + y[:, q:q + F]
            z_b = (y * wide).astype(bf16)
            zsum = dot(one_row, z_b)[0:1]
            d_basis = dot(wr, d_pre_b)
            d_dist = jnp.sum(d_basis * basis * off, axis=0, keepdims=True) * (-2.0 * sharp)
            dd_ref[pl.ds(e, 1), lanes] = d_dist + tan_ref[pl.ds(e, 1), lanes] * zsum
            gw1 = gw1 + dot(soft_b, d_raw_b, NT)
            gw2 = gw2 + dot(inputs, d_pre_b, NT)
        gf_ref[v] += dot(fold, jnp.concatenate(split(acc), axis=1), NT)
        gw_ref[0:9] += gw1.reshape(9, WROWS, F)
        gw_ref[9:11] += gw2.reshape(2, WROWS, F)
        return carry

    lax.fori_loop(0, count, body, 0)

    radial = dd_ref[...] / dist_ref[...]
    rrow = row_ref[0:1]
    srow = row_ref[1:2]
    t_sums = [jnp.zeros((48, F), f32), jnp.zeros((48, F), f32)]
    p_sums = [jnp.zeros((256, F), f32), jnp.zeros((256, F), f32)]
    for d in range(3):
        hi, lo = split(disp_ref[d] * radial)
        recv = dot(hi, rep4, NT) + dot(lo, rep4, NT)
        send = -(dot(hi, til4, NT) + dot(lo, til4, NT))
        put_u = (rrow // 8 * 16 + d == iota((48, ROWS), 0)).astype(bf16)
        put_v = (srow // 8 * 16 + d == iota((256, ROWS), 0)).astype(bf16)
        for k, mask in enumerate((in_low_u, in_up_u)):
            hi, lo = split(jnp.where(mask, recv, 0.0))
            t_sums[k] = t_sums[k] + dot(put_u, hi) + dot(put_u, lo)
        for k, mask in enumerate((in_low_v, in_up_v)):
            hi, lo = split(jnp.where(mask, send, 0.0))
            p_sums[k] = p_sums[k] + dot(put_v, hi) + dot(put_v, lo)
    for k in range(2):
        rows = pl.ds(16 * k, 16)
        tg_ref[:, rows, :] = t_sums[k].reshape(3, 16, F)
        pack_ref[:, pl.ds(ATOMS + 16 * k, 16), :] = p_sums[k].astype(bf16).reshape(BRICKS, 16, F)
    pack_ref[:, 0:ATOMS, :] = gf_ref[...].reshape(BRICKS, ATOMS, F).astype(bf16)
    gw_ref[11] = jnp.full((WROWS, F), count, jnp.int32).astype(f32)


def parts_of(x):
    hi = x.astype(bf16)
    rest = x - hi.astype(f32)
    mid = rest.astype(bf16)
    low = (rest - mid.astype(f32)).astype(bf16)
    return [hi, mid, low]


def pairs(count, tower_tiles, plate_tiles, shifts, tower, plate, w_rbf, b_rbf, w_filter, b_filter, chunk=256):
    padded = jnp.pad(jnp.stack([tower_tiles, plate_tiles, shifts]), ((0, 0), (0, ROWS - MAXT)))
    zeros = [jnp.zeros((F,), bf16)] * (NRBF - 3)
    w1 = jnp.concatenate([(w_rbf * 0.5).T, jnp.stack(parts_of(b_rbf * 0.5) + zeros, axis=1)], axis=1)
    nwft = jnp.concatenate([-w_filter.T, jnp.stack(parts_of(b_filter) + zeros, axis=1)], axis=1)
    smem = pl.BlockSpec(memory_space=pltpu.SMEM)
    vmem = pl.BlockSpec(memory_space=pltpu.VMEM)
    return pl.pallas_call(
        lambda *refs: pairs_kernel(*refs, chunk=chunk),
        out_shape=(
            jax.ShapeDtypeStruct((BRICKS, PACK, F), bf16),
            jax.ShapeDtypeStruct((3, 32, F), f32),
            jax.ShapeDtypeStruct((16, WROWS, F), f32),
        ),
        in_specs=[smem] * 3 + [vmem] * 8,
        out_specs=[vmem] * 3,
        scratch_shapes=[
            pltpu.VMEM((3, ROWS, PAIRS), f32),
            pltpu.VMEM((ROWS, PAIRS), f32),
            pltpu.VMEM((ROWS, PAIRS), f32),
            pltpu.VMEM((ROWS, PAIRS), f32),
            pltpu.VMEM((ROWS, PAIRS), f32),
            pltpu.VMEM((TILE, PAIRS), bf16),
            pltpu.VMEM((PLATE, TILE, F), f32),
        ],
        compiler_params=pltpu.CompilerParams(vmem_limit_bytes=40 << 20),
        name="pairs",
    )(count, tower_tiles, plate_tiles, tower, plate, padded.T, padded, w1, w_rbf, nwft, w_filter * jnp.asarray(0.5, bf16))


def send_to(src, dst, sends, recvs, slot, device):
    copy = pltpu.make_async_remote_copy(
        src_ref=src, dst_ref=dst, send_sem=sends.at[slot], recv_sem=recvs.at[slot],
        device_id=device, device_id_type=pl.DeviceIdType.MESH,
    )
    copy.start()
    return copy


def greet(devices):
    barrier = pltpu.get_barrier_semaphore()
    for device in devices:
        pl.semaphore_signal(barrier, inc=1, device_id=device, device_id_type=pl.DeviceIdType.MESH)
    pl.semaphore_wait(barrier, len(devices))


def gather_kernel(cnt_s, feat_ref, adj_ref, pos_ref, plate_ref, tower_ref, chip_send, chip_recv, mate_send, mate_recv, tower_send, tower_recv):
    t = lax.axis_index("tower")
    p = lax.axis_index("plate")
    q, core = p // 2, p % 2
    mate = (t, q * 2 + 1 - core)
    above = ((t + 1) % 16, p)
    below = ((t + 15) % 16, p)
    chips = [(q + d) % 8 for d in range(8)]
    back = [(q + 8 - d) % 8 for d in range(8)]
    live = iota((ATOMS, F), 0) < cnt_s[0]
    zero = jnp.zeros((13, F), bf16)
    for rows, ref, slot in ((feat_ref, plate_ref, p), (adj_ref, tower_ref, 1)):
        ref[slot, 0:ATOMS, :] = jnp.where(live, rows[...].astype(f32), 0.0).astype(bf16)
        for k in range(2):
            ref[slot, pl.ds(ATOMS + 16 * k, 16), :] = jnp.concatenate([pos_ref[:, k * F:(k + 1) * F].astype(f32), jnp.zeros((13, F), f32)], axis=0).astype(bf16)
    greet([(t, chips[d] * 2 + core) for d in range(1, 8)] + [mate, above, below])
    mine = plate_ref.at[p]
    out = [send_to(mine, mine, chip_send, chip_recv, d, (t, chips[d] * 2 + core)) for d in range(1, 8)]
    out.append(send_to(mine, mine, mate_send, mate_recv, 0, mate))
    up = send_to(tower_ref.at[1], tower_ref.at[0], tower_send, tower_recv, 0, above)
    down = send_to(tower_ref.at[1], tower_ref.at[2], tower_send, tower_recv, 1, below)
    passed = []
    for d in range(1, 8):
        out[d - 1].wait_recv()
        block = plate_ref.at[back[d] * 2 + core]
        passed.append(send_to(block, block, mate_send, mate_recv, d, mate))
    for copy in out:
        copy.wait_send()
    out[7].wait_recv()
    for copy in passed + [up, down]:
        copy.wait()


def gather(count, feat, adj, pos):
    smem = pl.BlockSpec(memory_space=pltpu.SMEM)
    vmem = pl.BlockSpec(memory_space=pltpu.VMEM)
    return pl.pallas_call(
        gather_kernel,
        out_shape=(jax.ShapeDtypeStruct((BRICKS, PACK, F), bf16), jax.ShapeDtypeStruct((3, PACK, F), bf16)),
        in_specs=[smem] + [vmem] * 3,
        out_specs=[vmem] * 2,
        scratch_shapes=[pltpu.SemaphoreType.DMA((8,))] * 4 + [pltpu.SemaphoreType.DMA((2,))] * 2,
        compiler_params=pltpu.CompilerParams(collective_id=0, has_side_effects=True, vmem_limit_bytes=24 << 20),
        name="gather",
    )(count, feat, adj, pos)


def reduce_kernel(
    cnt_s, pack_ref, tg_ref, gw_ref, gf_out, gp_out, wr_out, br_out, wf_out, bf_out,
    mate_buf, send_buf, chip_buf, tower_buf, w1_buf, w2_own, w2_buf, w3_buf,
    mate_send, mate_recv, chip_send, chip_recv, tower_send, tower_recv, w_send, w_recv,
):
    t = lax.axis_index("tower")
    p = lax.axis_index("plate")
    q, core = p // 2, p % 2
    mate = (t, q * 2 + 1 - core)
    chips = [(q + d) % 8 for d in range(8)]
    plate = [(t, (p + d) % 16) for d in range(16)]
    tower = [((t + d) % 16, p) for d in range(16)]
    greet(plate[1:] + tower[1:])
    first = [send_to(gw_ref.at[(p + d) % 16], w1_buf.at[d], w_send.at[0], w_recv.at[0], d, plate[d]) for d in range(1, 16)]
    halves = [send_to(pack_ref.at[chips[d] * 2 + 1 - core], mate_buf.at[d], mate_send, mate_recv, d, mate) for d in (1, 2, 3, 4, 5, 6, 7, 0)]
    up = send_to(tg_ref.at[2], tower_buf.at[0], tower_send, tower_recv, 0, tower[1])
    down = send_to(tg_ref.at[0], tower_buf.at[1], tower_send, tower_recv, 1, tower[15])
    total = gw_ref[p]
    for d in range(1, 16):
        first[d - 1].wait_recv()
        total = total + w1_buf[d]
    w2_own[...] = total
    second = [send_to(w2_own, w2_buf.at[d], w_send.at[1], w_recv.at[1], d, tower[d]) for d in range(1, 16)]
    chip = []
    for d in range(1, 8):
        halves[d - 1].wait_recv()
        send_buf[d] = (pack_ref[chips[d] * 2 + core].astype(f32) + mate_buf[d].astype(f32)).astype(bf16)
        chip.append(send_to(send_buf.at[d], chip_buf.at[d], chip_send, chip_recv, d, (t, chips[d] * 2 + core)))
    for d in range(1, 16):
        second[d - 1].wait_recv()
        total = total + w2_buf[d]
    w3_buf[p] = total
    third = [send_to(w3_buf.at[p], w3_buf.at[p], w_send.at[2], w_recv.at[2], d, plate[d]) for d in range(1, 16)]
    halves[7].wait_recv()
    acc = pack_ref[p].astype(f32) + mate_buf[0].astype(f32)
    for d in range(1, 8):
        chip[d - 1].wait_recv()
        acc = acc + chip_buf[d].astype(f32)
    gf_out[...] = jnp.where(iota((ATOMS, F), 0) < cnt_s[0], acc[0:ATOMS], 0.0)
    up.wait_recv()
    down.wait_recv()
    moved = acc[ATOMS:PACK] + tg_ref[1] + tower_buf[0] + tower_buf[1]
    for k in range(2):
        gp_out[:, k * F:(k + 1) * F] = moved[16 * k:16 * k + 3]
    for d in range(1, 16):
        third[d - 1].wait_recv()
    scale = lax.rsqrt(w3_buf[11][0:1] * (TILE * TILE))
    wf_out[...] = w3_buf[0:8].reshape(F, F) * -scale
    bf_out[...] = w3_buf[8][0:1] * scale
    wr_out[...] = w3_buf[9] * scale
    br_out[...] = w3_buf[10][0:1] * scale
    for copy in first + halves + [up, down] + second + chip + third:
        copy.wait_send()


def reduce(count, pack, tg, gw):
    smem = pl.BlockSpec(memory_space=pltpu.SMEM)
    vmem = pl.BlockSpec(memory_space=pltpu.VMEM)
    weights = pltpu.VMEM((16, WROWS, F), f32)
    dma = pltpu.SemaphoreType.DMA
    return pl.pallas_call(
        reduce_kernel,
        out_shape=(
            jax.ShapeDtypeStruct((ATOMS, F), f32), jax.ShapeDtypeStruct((3, ATOMS), f32), jax.ShapeDtypeStruct((NRBF, F), f32),
            jax.ShapeDtypeStruct((1, F), f32), jax.ShapeDtypeStruct((F, F), f32), jax.ShapeDtypeStruct((1, F), f32),
        ),
        in_specs=[smem] + [vmem] * 3,
        out_specs=[vmem] * 6,
        scratch_shapes=[pltpu.VMEM((8, PACK, F), bf16)] * 3 + [
            pltpu.VMEM((2, 32, F), f32), weights, pltpu.VMEM((WROWS, F), f32), weights, weights,
            dma((8,)), dma((8,)), dma((8,)), dma((8,)), dma((2,)), dma((2,)), dma((3, 16)), dma((3, 16)),
        ],
        compiler_params=pltpu.CompilerParams(collective_id=1, has_side_effects=True, vmem_limit_bytes=24 << 20),
        name="reduce",
    )(count, pack, tg, gw)


def local(features, adjoint, positions, w_rbf, b_rbf, w_filter, b_filter, atom_counts, tile_counts, tower_tiles, plate_tiles, image_shifts):
    plate, tower = gather(atom_counts[0], features[0], adjoint[0], positions[:, 0, :])
    pack, tg, gw = pairs(
        tile_counts[0], tower_tiles[0, 0], plate_tiles[0, 0], image_shifts[0, 0],
        tower, plate, w_rbf, b_rbf, w_filter, b_filter,
    )
    gf, gp, wr, br, wf, bf = reduce(atom_counts[0], pack, tg, gw)
    return gf[None], gp[:, None, :], wr, br[0], wf, bf[0]


def solution(mesh):
    from jax.sharding import PartitionSpec as P
    brick = P("tower", "plate", None)
    one = P("tower", "plate")
    return jax.shard_map(
        local, mesh=mesh,
        in_specs=(brick, brick, P(None, "tower", "plate"), P(), P(), P(), P(), one, one, brick, brick, brick),
        out_specs=(brick, P(None, "tower", "plate"), P(), P(), P(), P()),
        check_vma=False,
    )
```

```python
import math

import jax
import jax.numpy as jnp
from jax import lax
from jax.experimental import pallas as pl
from jax.experimental.pallas import tpu as pltpu

F = 128
TILE = 32
PAIRS = TILE * TILE
MAXT = 56
ATOMS = 256
PACK = ATOMS + 32
BRICKS = 16
WROWS = 16
ROWS = 64
TOWER = 24
PLATE = 128
NRBF = 16
cutoff = 3.0
soften = 0.01
sharp = 10.0
f32 = jnp.float32
bf16 = jnp.bfloat16

NN = (((1,), (0,)), ((), ()))
NT = (((1,), (1,)), ((), ()))
TN = (((0,), (0,)), ((), ()))


def dot(a, b, dims=NN):
    return lax.dot_general(a, b, dims, preferred_element_type=f32)


def iota(shape, axis):
    return lax.broadcasted_iota(jnp.int32, shape, axis)


def split(x):
    hi = x.astype(bf16)
    return hi, (x - hi.astype(f32)).astype(bf16)


def sine(x):
    y = x * x
    acc = jnp.full_like(x, 1.0 / 6227020800.0)
    for c in (-1.0 / 39916800.0, 1.0 / 362880.0, -1.0 / 5040.0, 1.0 / 120.0, -1.0 / 6.0, 1.0):
        acc = acc * y + c
    return acc * x


def three(x):
    hi = x.astype(bf16).astype(f32)
    mid = (x - hi).astype(bf16).astype(f32)
    return [hi, mid, x - hi - mid]


def pairs_kernel(
    cnt_s, u_s, v_s,
    tower_ref, plate_ref, u_ref, v_ref, c_ref,
    wr_ref, br_ref, wf_ref, bf_ref,
    pack_ref, tg_ref, gw_ref,
    disp_ref, dist_ref, env_ref, tan_ref, dd_ref, rep_ref, gf_ref, list_ref,
    *, chunk, tiles,
):
    count = cnt_s[0, 0]
    list_ref[...] = jnp.zeros(list_ref.shape, f32)
    for k, ref in enumerate((u_ref, v_ref, c_ref)):
        list_ref[k:k + 1, 0:MAXT] = ref[0].astype(f32)
    lists = list_ref[...]
    columns = lists.T.astype(jnp.int32)
    rrow = lists[0:1, 0:ROWS].astype(jnp.int32)
    srow = lists[1:2, 0:ROWS].astype(jnp.int32)
    ucol = columns[0:ROWS, 0:1]
    vcol = columns[0:ROWS, 1:2]
    ccol = columns[0:ROWS, 2:3]
    rep = (iota((TILE, PAIRS), 1) >> 5 == iota((TILE, PAIRS), 0)).astype(bf16)
    rep_ref[...] = rep
    rep4 = (iota((F, PAIRS), 1) >> 5 == (iota((F, PAIRS), 0) & 31)).astype(bf16)
    til4 = ((iota((F, PAIRS), 1) & 31) == (iota((F, PAIRS), 0) & 31)).astype(bf16)
    group = iota((ROWS, F), 1) >> 5
    in_low_u, in_up_u = group == (ucol & 7), group + 4 == (ucol & 7)
    in_low_v, in_up_v = group == (vcol & 7), group + 4 == (vcol & 7)
    t_low = tower_ref[:, ATOMS:ATOMS + 16, :].reshape(48, F)
    t_up = tower_ref[:, ATOMS + 16:ATOMS + 32, :].reshape(48, F)
    p_low = plate_ref[:, ATOMS:ATOMS + 16, :].reshape(256, F)
    p_up = plate_ref[:, ATOMS + 16:ATOMS + 32, :].reshape(256, F)
    third = (ccol >= 3).astype(jnp.int32) + (ccol >= 6).astype(jnp.int32)
    shifts = (third - 1, ccol - 3 * third - 1, (ucol >> 3) - 1)
    square = jnp.zeros((ROWS, PAIRS), f32)
    for d in range(3):
        pick_u = ((ucol >> 3) * 16 + d == iota((ROWS, 48), 1)).astype(bf16)
        pick_v = ((vcol >> 3) * 16 + d == iota((ROWS, 256), 1)).astype(bf16)
        recv = jnp.where(in_low_u, dot(pick_u, t_low), 0.0) + jnp.where(in_up_u, dot(pick_u, t_up), 0.0)
        send = jnp.where(in_low_v, dot(pick_v, p_low), 0.0) + jnp.where(in_up_v, dot(pick_v, p_up), 0.0)
        disp = dot(recv.astype(bf16), rep4) - dot(send.astype(bf16), til4) + shifts[d].astype(f32)
        disp_ref[d] = disp
        square = square + disp * disp
    dist = jnp.sqrt(square + soften)
    dist_ref[...] = dist
    inside = (dist < cutoff) & (iota((ROWS, PAIRS), 0) < count)
    theta = jnp.minimum(dist, cutoff) * (math.pi / (2 * cutoff))
    cosine = jnp.maximum(sine(math.pi / 2 - theta), 1e-6)
    env_ref[...] = jnp.where(inside, cosine * cosine, 0.0)
    tan_ref[...] = jnp.where(inside, (-math.pi / cutoff) * sine(theta) / cosine, 0.0)
    dd_ref[...] = jnp.zeros((ROWS, PAIRS), f32)
    gf_ref[...] = jnp.zeros(gf_ref.shape, f32)
    gw_ref[...] = jnp.zeros(gw_ref.shape, f32)

    centres = iota((NRBF, 1), 0).astype(f32) * (cutoff / (NRBF - 1))
    ones = jnp.ones((NRBF, chunk), bf16)
    wr = wr_ref[...]
    zeros = jnp.zeros((NRBF - 3, F), f32)
    w1 = jnp.concatenate([wr.astype(f32) * 0.5] + three(br_ref[...] * 0.5) + [zeros], axis=0).T.astype(bf16)
    wf = wf_ref[...].astype(f32)
    nwft = jnp.concatenate([-wf.T, jnp.concatenate(three(bf_ref[...]) + [zeros], axis=0).T], axis=1).astype(bf16)
    hwf = (wf * 0.5).astype(bf16)
    fold = ((iota((TILE, 2 * F), 1) & 31) == iota((TILE, 2 * F), 0)).astype(bf16)
    one_row = jnp.ones((NRBF, F), bf16)

    def body(step, carry):
        entries = [step * tiles + k for k in range(tiles)]
        streams = []
        for e in entries:
            u = u_s[0, 0, e]
            v = v_s[0, 0, e]
            adj = tower_ref[u >> 3, pl.ds(pl.multiple_of((u & 7) * TILE, TILE), TILE), :]
            adj = jnp.concatenate([adj] * 2, axis=0)
            feat = plate_ref[v >> 3, pl.ds(pl.multiple_of((v & 7) * TILE, TILE), TILE), :].astype(f32)
            feat4 = jnp.concatenate([feat] * 4, axis=0).T
            wide = jnp.concatenate([feat4] * (chunk // F), axis=1)
            for s in range(0, PAIRS, chunk):
                streams.append(dict(e=e, v=v, adj=adj, wide=wide, lanes=pl.ds(s, chunk)))
        for x in streams:
            x['off'] = dist_ref[pl.ds(x['e'], 1), x['lanes']] - centres
            x['basis'] = jnp.exp(-sharp * x['off'] * x['off'])
            x['inputs'] = jnp.concatenate([x['basis'].astype(bf16), ones], axis=0)
            x['half'] = dot(w1, x['inputs'])
            hi, lo = split(env_ref[pl.ds(x['e'], 1), x['lanes']])
            member = rep_ref[:, x['lanes']]
            spread = jnp.concatenate([member * hi, member * lo], axis=0)
            x['adj_env'] = dot(x['adj'], spread, TN)
        for x in streams:
            x['t'] = jnp.tanh(x['half'])
            x['soft_b'] = jnp.concatenate([jnp.log(1.0 - x['t']).astype(bf16), ones], axis=0)
            x['d_raw_b'] = (x['adj_env'] * x['wide']).astype(bf16)
        for x in streams:
            x['filt'] = dot(nwft, x['soft_b'])
            x['d_soft'] = dot(hwf, x['d_raw_b'])
        for x in streams:
            x['d_pre_b'] = (x['d_soft'] * (1.0 + x['t'])).astype(bf16)
            x['y'] = x['adj_env'] * x['filt']
            x['z_b'] = (x['y'] * x['wide']).astype(bf16)
        gw1 = jnp.zeros((F + NRBF, F), f32)
        gw2 = jnp.zeros((2 * NRBF, F), f32)
        for x in streams:
            zsum = dot(one_row, x['z_b'])[0:1]
            d_basis = dot(wr, x['d_pre_b'])
            d_dist = jnp.sum(d_basis * x['basis'] * x['off'], axis=0, keepdims=True) * (-2.0 * sharp)
            x['dd'] = d_dist + tan_ref[pl.ds(x['e'], 1), x['lanes']] * zsum
            gw1 = gw1 + dot(x['soft_b'], x['d_raw_b'], NT)
            gw2 = gw2 + dot(x['inputs'], x['d_pre_b'], NT)
        for e in entries:
            acc = jnp.zeros((F, F), f32)
            for x in streams:
                if x['e'] is e:
                    v = x['v']
                    dd_ref[pl.ds(e, 1), x['lanes']] = x['dd']
                    for q in range(0, chunk, F):
                        acc = acc + x['y'][:, q:q + F]
            gf_ref[v] += dot(fold, jnp.concatenate(split(acc), axis=1), NT)
        gw_ref[0:9] += gw1.reshape(9, WROWS, F)
        gw_ref[9:11] += gw2.reshape(2, WROWS, F)
        return carry

    lax.fori_loop(0, (count + tiles - 1) // tiles, body, 0)

    radial = dd_ref[...] / dist_ref[...]
    t_sums = [jnp.zeros((48, F), f32), jnp.zeros((48, F), f32)]
    p_sums = [jnp.zeros((256, F), f32), jnp.zeros((256, F), f32)]
    for d in range(3):
        hi, lo = split(disp_ref[d] * radial)
        recv = dot(hi, rep4, NT) + dot(lo, rep4, NT)
        send = -(dot(hi, til4, NT) + dot(lo, til4, NT))
        put_u = ((rrow >> 3) * 16 + d == iota((48, ROWS), 0)).astype(bf16)
        put_v = ((srow >> 3) * 16 + d == iota((256, ROWS), 0)).astype(bf16)
        for k, mask in enumerate((in_low_u, in_up_u)):
            hi, lo = split(jnp.where(mask, recv, 0.0))
            t_sums[k] = t_sums[k] + dot(put_u, hi) + dot(put_u, lo)
        for k, mask in enumerate((in_low_v, in_up_v)):
            hi, lo = split(jnp.where(mask, send, 0.0))
            p_sums[k] = p_sums[k] + dot(put_v, hi) + dot(put_v, lo)
    for k in range(2):
        rows = pl.ds(16 * k, 16)
        tg_ref[:, rows, :] = t_sums[k].reshape(3, 16, F)
        pack_ref[:, pl.ds(ATOMS + 16 * k, 16), :] = p_sums[k].astype(bf16).reshape(BRICKS, 16, F)
    pack_ref[:, 0:ATOMS, :] = gf_ref[...].reshape(BRICKS, ATOMS, F).astype(bf16)
    gw_ref[11] = jnp.full((WROWS, F), count, jnp.int32).astype(f32)


def pairs(count, tower_tiles, plate_tiles, shifts, tower, plate, w_rbf, b_rbf, w_filter, b_filter, chunk=256, tiles=2):
    smem = pl.BlockSpec(memory_space=pltpu.SMEM)
    vmem = pl.BlockSpec(memory_space=pltpu.VMEM)
    return pl.pallas_call(
        lambda *refs: pairs_kernel(*refs, chunk=chunk, tiles=tiles),
        out_shape=(
            jax.ShapeDtypeStruct((BRICKS, PACK, F), bf16),
            jax.ShapeDtypeStruct((3, 32, F), f32),
            jax.ShapeDtypeStruct((16, WROWS, F), f32),
        ),
        in_specs=[smem] * 3 + [vmem] * 9,
        out_specs=[vmem] * 3,
        scratch_shapes=[
            pltpu.VMEM((3, ROWS, PAIRS), f32),
            pltpu.VMEM((ROWS, PAIRS), f32),
            pltpu.VMEM((ROWS, PAIRS), f32),
            pltpu.VMEM((ROWS, PAIRS), f32),
            pltpu.VMEM((ROWS, PAIRS), f32),
            pltpu.VMEM((TILE, PAIRS), bf16),
            pltpu.VMEM((PLATE, TILE, F), f32),
            pltpu.VMEM((8, F), f32),
        ],
        compiler_params=pltpu.CompilerParams(vmem_limit_bytes=48 << 20),
        name="pairs",
    )(count, tower_tiles, plate_tiles, tower, plate, tower_tiles, plate_tiles, shifts, w_rbf, b_rbf.reshape(1, F), w_filter, b_filter.reshape(1, F))


def send_to(src, dst, sends, recvs, slot, device):
    copy = pltpu.make_async_remote_copy(
        src_ref=src, dst_ref=dst, send_sem=sends.at[slot], recv_sem=recvs.at[slot],
        device_id=device, device_id_type=pl.DeviceIdType.MESH,
    )
    copy.start()
    return copy


def greet(devices):
    barrier = pltpu.get_barrier_semaphore()
    for device in devices:
        pl.semaphore_signal(barrier, inc=1, device_id=device, device_id_type=pl.DeviceIdType.MESH)
    pl.semaphore_wait(barrier, len(devices))


def gather_kernel(cnt_s, feat_ref, adj_ref, pos_ref, plate_ref, tower_ref, chip_send, chip_recv, mate_send, mate_recv, tower_send, tower_recv):
    t = lax.axis_index("tower")
    p = lax.axis_index("plate")
    q, core = p // 2, p % 2
    mate = (t, q * 2 + 1 - core)
    above = ((t + 1) % 16, p)
    below = ((t + 15) % 16, p)
    chips = [(q + d) % 8 for d in range(8)]
    back = [(q + 8 - d) % 8 for d in range(8)]
    live = iota((ATOMS, F), 0) < cnt_s[0]
    zero = jnp.zeros((13, F), bf16)
    for rows, ref, slot in ((feat_ref, plate_ref, p), (adj_ref, tower_ref, 1)):
        ref[slot, 0:ATOMS, :] = jnp.where(live, rows[...].astype(f32), 0.0).astype(bf16)
        for k in range(2):
            ref[slot, pl.ds(ATOMS + 16 * k, 16), :] = jnp.concatenate([pos_ref[:, k * F:(k + 1) * F].astype(f32), jnp.zeros((13, F), f32)], axis=0).astype(bf16)
    greet([(t, chips[d] * 2 + core) for d in range(1, 8)] + [mate, above, below])
    mine = plate_ref.at[p]
    out = [send_to(mine, mine, chip_send, chip_recv, d, (t, chips[d] * 2 + core)) for d in range(1, 8)]
    out.append(send_to(mine, mine, mate_send, mate_recv, 0, mate))
    up = send_to(tower_ref.at[1], tower_ref.at[0], tower_send, tower_recv, 0, above)
    down = send_to(tower_ref.at[1], tower_ref.at[2], tower_send, tower_recv, 1, below)
    passed = []
    for d in range(1, 8):
        out[d - 1].wait_recv()
        block = plate_ref.at[back[d] * 2 + core]
        passed.append(send_to(block, block, mate_send, mate_recv, d, mate))
    for copy in out:
        copy.wait_send()
    out[7].wait_recv()
    for copy in passed + [up, down]:
        copy.wait()


def gather(count, feat, adj, pos):
    smem = pl.BlockSpec(memory_space=pltpu.SMEM)
    vmem = pl.BlockSpec(memory_space=pltpu.VMEM)
    return pl.pallas_call(
        gather_kernel,
        out_shape=(jax.ShapeDtypeStruct((BRICKS, PACK, F), bf16), jax.ShapeDtypeStruct((3, PACK, F), bf16)),
        in_specs=[smem] + [vmem] * 3,
        out_specs=[vmem] * 2,
        scratch_shapes=[pltpu.SemaphoreType.DMA((8,))] * 4 + [pltpu.SemaphoreType.DMA((2,))] * 2,
        compiler_params=pltpu.CompilerParams(collective_id=0, has_side_effects=True, vmem_limit_bytes=24 << 20),
        name="gather",
    )(count, feat, adj, pos)


def reduce_kernel(
    cnt_s, pack_ref, tg_ref, gw_ref, gf_out, gp_out, wr_out, br_out, wf_out, bf_out,
    mate_buf, send_buf, chip_buf, tower_buf, w1_buf, w2_own, w2_buf, w3_buf,
    mate_send, mate_recv, chip_send, chip_recv, tower_send, tower_recv, w_send, w_recv,
):
    t = lax.axis_index("tower")
    p = lax.axis_index("plate")
    q, core = p // 2, p % 2
    mate = (t, q * 2 + 1 - core)
    chips = [(q + d) % 8 for d in range(8)]
    plate = [(t, (p + d) % 16) for d in range(16)]
    tower = [((t + d) % 16, p) for d in range(16)]
    greet(plate[1:] + tower[1:])
    first = [send_to(gw_ref.at[(p + d) % 16], w1_buf.at[d], w_send.at[0], w_recv.at[0], d, plate[d]) for d in range(1, 16)]
    halves = [send_to(pack_ref.at[chips[d] * 2 + 1 - core], mate_buf.at[d], mate_send, mate_recv, d, mate) for d in (1, 2, 3, 4, 5, 6, 7, 0)]
    up = send_to(tg_ref.at[2], tower_buf.at[0], tower_send, tower_recv, 0, tower[1])
    down = send_to(tg_ref.at[0], tower_buf.at[1], tower_send, tower_recv, 1, tower[15])
    total = gw_ref[p]
    for d in range(1, 16):
        first[d - 1].wait_recv()
        total = total + w1_buf[d]
    w2_own[...] = total
    second = [send_to(w2_own, w2_buf.at[d], w_send.at[1], w_recv.at[1], d, tower[d]) for d in range(1, 16)]
    chip = []
    for d in range(1, 8):
        halves[d - 1].wait_recv()
        send_buf[d] = (pack_ref[chips[d] * 2 + core].astype(f32) + mate_buf[d].astype(f32)).astype(bf16)
        chip.append(send_to(send_buf.at[d], chip_buf.at[d], chip_send, chip_recv, d, (t, chips[d] * 2 + core)))
    for d in range(1, 16):
        second[d - 1].wait_recv()
        total = total + w2_buf[d]
    w3_buf[p] = total
    third = [send_to(w3_buf.at[p], w3_buf.at[p], w_send.at[2], w_recv.at[2], d, plate[d]) for d in range(1, 16)]
    halves[7].wait_recv()
    acc = pack_ref[p].astype(f32) + mate_buf[0].astype(f32)
    for d in range(1, 8):
        chip[d - 1].wait_recv()
        acc = acc + chip_buf[d].astype(f32)
    gf_out[...] = jnp.where(iota((ATOMS, F), 0) < cnt_s[0], acc[0:ATOMS], 0.0)
    up.wait_recv()
    down.wait_recv()
    moved = acc[ATOMS:PACK] + tg_ref[1] + tower_buf[0] + tower_buf[1]
    for k in range(2):
        gp_out[:, k * F:(k + 1) * F] = moved[16 * k:16 * k + 3]
    for d in range(1, 16):
        third[d - 1].wait_recv()
    scale = lax.rsqrt(w3_buf[11][0:1] * (TILE * TILE))
    wf_out[...] = w3_buf[0:8].reshape(F, F) * -scale
    bf_out[...] = w3_buf[8][0:1] * scale
    wr_out[...] = w3_buf[9] * scale
    br_out[...] = w3_buf[10][0:1] * scale
    for copy in first + halves + [up, down] + second + chip + third:
        copy.wait_send()


def reduce(count, pack, tg, gw):
    smem = pl.BlockSpec(memory_space=pltpu.SMEM)
    vmem = pl.BlockSpec(memory_space=pltpu.VMEM)
    weights = pltpu.VMEM((16, WROWS, F), f32)
    dma = pltpu.SemaphoreType.DMA
    return pl.pallas_call(
        reduce_kernel,
        out_shape=(
            jax.ShapeDtypeStruct((ATOMS, F), f32), jax.ShapeDtypeStruct((3, ATOMS), f32), jax.ShapeDtypeStruct((NRBF, F), f32),
            jax.ShapeDtypeStruct((1, F), f32), jax.ShapeDtypeStruct((F, F), f32), jax.ShapeDtypeStruct((1, F), f32),
        ),
        in_specs=[smem] + [vmem] * 3,
        out_specs=[vmem] * 6,
        scratch_shapes=[pltpu.VMEM((8, PACK, F), bf16)] * 3 + [
            pltpu.VMEM((2, 32, F), f32), weights, pltpu.VMEM((WROWS, F), f32), weights, weights,
            dma((8,)), dma((8,)), dma((8,)), dma((8,)), dma((2,)), dma((2,)), dma((3, 16)), dma((3, 16)),
        ],
        compiler_params=pltpu.CompilerParams(collective_id=1, has_side_effects=True, vmem_limit_bytes=24 << 20),
        name="reduce",
    )(count, pack, tg, gw)


def local(features, adjoint, positions, w_rbf, b_rbf, w_filter, b_filter, atom_counts, tile_counts, tower_tiles, plate_tiles, image_shifts):
    plate, tower = gather(atom_counts[0], features[0], adjoint[0], positions[:, 0, :])
    pack, tg, gw = pairs(
        tile_counts, tower_tiles, plate_tiles, image_shifts,
        tower, plate, w_rbf, b_rbf, w_filter, b_filter,
    )
    gf, gp, wr, br, wf, bf = reduce(atom_counts[0], pack, tg, gw)
    return gf[None], gp[:, None, :], wr, br[0], wf, bf[0]


def solution(mesh):
    from jax.sharding import PartitionSpec as P
    brick = P("tower", "plate", None)
    one = P("tower", "plate")
    return jax.shard_map(
        local, mesh=mesh,
        in_specs=(brick, brick, P(None, "tower", "plate"), P(), P(), P(), P(), one, one, brick, brick, brick),
        out_specs=(brick, P(None, "tower", "plate"), P(), P(), P(), P()),
        check_vma=False,
    )
```

```python
import math

import jax
import jax.numpy as jnp
from jax import lax
from jax.experimental import pallas as pl
from jax.experimental.pallas import tpu as pltpu

F = 128
TILE = 32
PAIRS = TILE * TILE
MAXT = 56
ATOMS = 256
PACK = ATOMS + 16
BRICKS = 16
WROWS = 16
ROWS = 64
TOWER = 24
PLATE = 128
NRBF = 16
cutoff = 3.0
soften = 0.01
sharp = 10.0
f32 = jnp.float32
bf16 = jnp.bfloat16

NN = (((1,), (0,)), ((), ()))
NT = (((1,), (1,)), ((), ()))
TN = (((0,), (0,)), ((), ()))


def dot(a, b, dims=NN):
    return lax.dot_general(a, b, dims, preferred_element_type=f32)


def iota(shape, axis):
    return lax.broadcasted_iota(jnp.int32, shape, axis)


def split(x):
    hi = x.astype(bf16)
    return hi, (x - hi.astype(f32)).astype(bf16)


def sine(x):
    y = x * x
    acc = jnp.full_like(x, 1.0 / 6227020800.0)
    for c in (-1.0 / 39916800.0, 1.0 / 362880.0, -1.0 / 5040.0, 1.0 / 120.0, -1.0 / 6.0, 1.0):
        acc = acc * y + c
    return acc * x


def three(x):
    hi = x.astype(bf16).astype(f32)
    mid = (x - hi).astype(bf16).astype(f32)
    return [hi, mid, x - hi - mid]


def pairs_kernel(
    cnt_s,
    tower_ref, plate_ref, u_ref, v_ref, c_ref,
    wr_ref, br_ref, wf_ref, bf_ref,
    pack_ref, tg_ref, gw_ref,
    disp_ref, dist_ref, env_ref, tan_ref, dd_ref, rep_ref, gf_ref, list_ref, sum_ref, u_s, v_s, list_sem,
    *, chunk, tiles,
):
    count = cnt_s[0, 0]
    lists_in = [pltpu.make_async_copy(u_ref, u_s, list_sem.at[0]), pltpu.make_async_copy(v_ref, v_s, list_sem.at[1])]
    for copy in lists_in:
        copy.start()
    list_ref[...] = jnp.zeros(list_ref.shape, f32)
    for k, ref in enumerate((u_ref, v_ref, c_ref)):
        list_ref[k:k + 1, 0:MAXT] = ref[0].astype(f32)
    lists = list_ref[...]
    columns = lists.T.astype(jnp.int32)
    rrow = lists[0:1, 0:ROWS].astype(jnp.int32)
    srow = lists[1:2, 0:ROWS].astype(jnp.int32)
    ucol = columns[0:ROWS, 0:1]
    vcol = columns[0:ROWS, 1:2]
    ccol = columns[0:ROWS, 2:3]
    rep = (iota((TILE, PAIRS), 1) >> 5 == iota((TILE, PAIRS), 0)).astype(bf16)
    rep_ref[...] = rep
    rep4 = (iota((F, PAIRS), 1) >> 5 == (iota((F, PAIRS), 0) & 31)).astype(bf16)
    til4 = ((iota((F, PAIRS), 1) & 31) == (iota((F, PAIRS), 0) & 31)).astype(bf16)
    group = iota((ROWS, F), 1) >> 5
    in_u = group == (ucol & 3)
    in_v = group == (vcol & 3)
    row_u = (ucol >> 3) * 16 + ((ucol >> 2) & 1) * 3
    row_v = (vcol >> 3) * 16 + ((vcol >> 2) & 1) * 3
    t_pos = tower_ref[:, ATOMS:PACK, :].reshape(48, F)
    p_pos = plate_ref[:, ATOMS:PACK, :].reshape(256, F)
    third = (ccol >= 3).astype(jnp.int32) + (ccol >= 6).astype(jnp.int32)
    shifts = (third - 1, ccol - 3 * third - 1, (ucol >> 3) - 1)
    square = jnp.zeros((ROWS, PAIRS), f32)
    for d in range(3):
        pick_u = (row_u + d == iota((ROWS, 48), 1)).astype(bf16)
        pick_v = (row_v + d == iota((ROWS, 256), 1)).astype(bf16)
        recv = jnp.where(in_u, dot(pick_u, t_pos), 0.0)
        send = jnp.where(in_v, dot(pick_v, p_pos), 0.0)
        disp = dot(recv.astype(bf16), rep4) - dot(send.astype(bf16), til4) + shifts[d].astype(f32)
        disp_ref[d] = disp
        square = square + disp * disp
    dist = jnp.sqrt(square + soften)
    dist_ref[...] = dist
    inside = (dist < cutoff) & (iota((ROWS, PAIRS), 0) < count)
    theta = jnp.minimum(dist, cutoff) * (math.pi / (2 * cutoff))
    cosine = jnp.maximum(sine(math.pi / 2 - theta), 1e-6)
    env_ref[...] = jnp.where(inside, cosine * cosine, 0.0)
    tan_ref[...] = jnp.where(inside, (-math.pi / cutoff) * sine(theta) / cosine, 0.0)
    dd_ref[...] = jnp.zeros((ROWS, PAIRS), f32)
    gf_ref[...] = jnp.zeros(gf_ref.shape, f32)
    sum_ref[...] = jnp.zeros(sum_ref.shape, f32)

    centres = iota((NRBF, 1), 0).astype(f32) * (cutoff / (NRBF - 1))
    ones = jnp.ones((NRBF, chunk), bf16)
    wr = wr_ref[...]
    zeros = jnp.zeros((NRBF - 3, F), f32)
    w1 = jnp.concatenate([wr.astype(f32) * 0.5] + three(br_ref[...] * 0.5) + [zeros], axis=0).T.astype(bf16)
    wf = wf_ref[...].astype(f32)
    nwft = jnp.concatenate([-wf.T, jnp.concatenate(three(bf_ref[...]) + [zeros], axis=0).T], axis=1).astype(bf16)
    hwf = (wf * 0.5).astype(bf16)
    fold = ((iota((TILE, 2 * F), 1) & 31) == iota((TILE, 2 * F), 0)).astype(bf16)

    def body(step, carry):
        entries = [step * tiles + k for k in range(tiles)]
        streams = []
        for e in entries:
            listed = jnp.minimum(e, MAXT - 1)
            u = u_s[0, 0, listed]
            v = v_s[0, 0, listed]
            adj = tower_ref[u >> 3, pl.ds(pl.multiple_of((u & 7) * TILE, TILE), TILE), :]
            adj = jnp.concatenate([adj] * 2, axis=0)
            feat = plate_ref[v >> 3, pl.ds(pl.multiple_of((v & 7) * TILE, TILE), TILE), :].astype(f32)
            feat4 = jnp.concatenate([feat] * 4, axis=0).T
            wide = jnp.concatenate([feat4] * (chunk // F), axis=1)
            for s in range(0, PAIRS, chunk):
                streams.append(dict(e=e, v=v, adj=adj, wide=wide, lanes=pl.ds(s, chunk)))
        for x in streams:
            x['off'] = dist_ref[pl.ds(x['e'], 1), x['lanes']] - centres
            x['basis'] = jnp.exp(-sharp * x['off'] * x['off'])
            x['inputs'] = jnp.concatenate([x['basis'].astype(bf16), ones], axis=0)
            x['half'] = dot(w1, x['inputs'])
            hi, lo = split(env_ref[pl.ds(x['e'], 1), x['lanes']])
            member = rep_ref[:, x['lanes']]
            spread = jnp.concatenate([member * hi, member * lo], axis=0)
            x['adj_env'] = dot(x['adj'], spread, TN)
        for x in streams:
            x['t'] = jnp.tanh(x['half'])
            x['soft_b'] = jnp.concatenate([jnp.log(1.0 - x['t']).astype(bf16), ones], axis=0)
            x['d_raw_b'] = (x['adj_env'] * x['wide']).astype(bf16)
        for x in streams:
            x['filt'] = dot(nwft, x['soft_b'])
            x['d_soft'] = dot(hwf, x['d_raw_b'])
        for x in streams:
            x['d_pre_b'] = (x['d_soft'] * (1.0 + x['t'])).astype(bf16)
            x['y'] = x['adj_env'] * x['filt']
            x['zsum'] = jnp.sum(x['y'] * x['wide'], axis=0, keepdims=True)
        gw = jnp.zeros((2 * F, F + 2 * NRBF), f32)
        for x in streams:
            d_basis = dot(wr, x['d_pre_b'])
            d_dist = jnp.sum(d_basis * x['basis'] * x['off'], axis=0, keepdims=True) * (-2.0 * sharp)
            x['dd'] = d_dist + tan_ref[pl.ds(x['e'], 1), x['lanes']] * x['zsum']
            grads = jnp.concatenate([x['d_raw_b'], x['d_pre_b']], axis=0)
            values = jnp.concatenate([x['soft_b'], x['inputs'][0:NRBF]], axis=0)
            gw = gw + dot(grads, values, NT)
        for e in entries:
            acc = jnp.zeros((F, F), f32)
            for x in streams:
                if x['e'] is e:
                    v = x['v']
                    dd_ref[pl.ds(e, 1), x['lanes']] = x['dd']
                    for q in range(0, chunk, F):
                        acc = acc + x['y'][:, q:q + F]
            gf_ref[v] += dot(fold, jnp.concatenate(split(acc), axis=1), NT)
        sum_ref[...] += gw
        return carry

    for copy in lists_in:
        copy.wait()
    lax.fori_loop(0, (count + tiles - 1) // tiles, body, 0)

    radial = dd_ref[...] / dist_ref[...]
    t_sum = jnp.zeros((48, F), f32)
    p_sum = jnp.zeros((256, F), f32)
    to_u = (rrow >> 3) * 16 + ((rrow >> 2) & 1) * 3
    to_v = (srow >> 3) * 16 + ((srow >> 2) & 1) * 3
    for d in range(3):
        hi, lo = split(disp_ref[d] * radial)
        recv_hi, recv_lo = split(jnp.where(in_u, dot(hi, rep4, NT) + dot(lo, rep4, NT), 0.0))
        send_hi, send_lo = split(jnp.where(in_v, dot(hi, til4, NT) + dot(lo, til4, NT), 0.0))
        put_u = (to_u + d == iota((48, ROWS), 0)).astype(bf16)
        put_v = (to_v + d == iota((256, ROWS), 0)).astype(bf16)
        t_sum = t_sum + dot(put_u, recv_hi) + dot(put_u, recv_lo)
        p_sum = p_sum - dot(put_v, send_hi) - dot(put_v, send_lo)
    tg_ref[...] = t_sum.reshape(3, 16, F)
    pack_ref[:, ATOMS:PACK, :] = p_sum.astype(bf16).reshape(BRICKS, 16, F)
    pack_ref[:, 0:ATOMS, :] = gf_ref[...].reshape(BRICKS, ATOMS, F).astype(bf16)
    gw_ref[0:8] = sum_ref[0:F, 0:F].T.reshape(8, WROWS, F)
    gw_ref[8] = sum_ref[0:F, F:F + 2 * NRBF].T[0:WROWS]
    rest = sum_ref[F:2 * F, F:F + 2 * NRBF].T
    gw_ref[9] = rest[NRBF:2 * NRBF]
    gw_ref[10] = rest[0:NRBF]
    gw_ref[12:16] = jnp.zeros((4, WROWS, F), f32)
    gw_ref[11] = jnp.full((WROWS, F), count, jnp.int32).astype(f32)


def pairs(count, tower, plate, params, chunk=256, tiles=2):
    smem = pl.BlockSpec(memory_space=pltpu.SMEM)
    vmem = pl.BlockSpec(memory_space=pltpu.VMEM)
    return pl.pallas_call(
        lambda *refs: pairs_kernel(*refs, chunk=chunk, tiles=tiles),
        out_shape=(
            jax.ShapeDtypeStruct((BRICKS, PACK, F), bf16),
            jax.ShapeDtypeStruct((3, 16, F), f32),
            jax.ShapeDtypeStruct((16, WROWS, F), f32),
        ),
        in_specs=[smem] + [vmem] * 9,
        out_specs=[vmem] * 3,
        scratch_shapes=[
            pltpu.VMEM((3, ROWS, PAIRS), f32),
            pltpu.VMEM((ROWS, PAIRS), f32),
            pltpu.VMEM((ROWS, PAIRS), f32),
            pltpu.VMEM((ROWS, PAIRS), f32),
            pltpu.VMEM((ROWS, PAIRS), f32),
            pltpu.VMEM((TILE, PAIRS), bf16),
            pltpu.VMEM((PLATE, TILE, F), f32),
            pltpu.VMEM((8, F), f32),
            pltpu.VMEM((2 * F, F + 2 * NRBF), f32),
            pltpu.SMEM((1, 1, MAXT), jnp.int32),
            pltpu.SMEM((1, 1, MAXT), jnp.int32),
            pltpu.SemaphoreType.DMA((2,)),
        ],
        compiler_params=pltpu.CompilerParams(vmem_limit_bytes=48 << 20),
        name="pairs",
    )(count, tower, plate, *params)


def send_to(src, dst, sends, recvs, slot, device):
    copy = pltpu.make_async_remote_copy(
        src_ref=src, dst_ref=dst, send_sem=sends.at[slot], recv_sem=recvs.at[slot],
        device_id=device, device_id_type=pl.DeviceIdType.MESH,
    )
    copy.start()
    return copy


def greet(devices):
    barrier = pltpu.get_barrier_semaphore()
    for device in devices:
        pl.semaphore_signal(barrier, inc=1, device_id=device, device_id_type=pl.DeviceIdType.MESH)
    pl.semaphore_wait(barrier, len(devices))


def gather_kernel(
    cnt_s, feat_hbm, adj_hbm, pos_hbm, *refs,
):
    params_hbm, (plate_ref, tower_ref), params = refs[:7], refs[7:9], refs[9:16]
    feat_ref, adj_ref, pos_ref, local_sem, chip_send, chip_recv, mate_send, mate_recv, tower_send, tower_recv = refs[16:]
    t = lax.axis_index("tower")
    p = lax.axis_index("plate")
    q, core = p // 2, p % 2
    mate = (t, q * 2 + 1 - core)
    above = ((t + 1) % 16, p)
    below = ((t + 15) % 16, p)
    chips = [(q + d) % 8 for d in range(8)]
    back = [(q + 8 - d) % 8 for d in range(8)]
    local = []
    for k, (src, dst) in enumerate(zip((feat_hbm, adj_hbm, pos_hbm) + params_hbm, (feat_ref, adj_ref, pos_ref) + params)):
        local.append(pltpu.make_async_copy(src, dst, local_sem.at[k]))
        local[k].start()
    barrier = pltpu.get_barrier_semaphore()
    peers = [(t, chips[d] * 2 + core) for d in range(1, 8)] + [mate, above, below]
    for device in peers:
        pl.semaphore_signal(barrier, inc=1, device_id=device, device_id_type=pl.DeviceIdType.MESH)
    local[0].wait()
    local[1].wait()
    local[2].wait()
    live = iota((ATOMS, F), 0) < cnt_s[0, 0]
    halves = [pos_ref[:, k * F:(k + 1) * F].astype(f32) for k in range(2)]
    rows = jnp.concatenate(halves + [jnp.zeros((10, F), f32)], axis=0).astype(bf16)
    for src, ref, slot in ((feat_ref, plate_ref, p), (adj_ref, tower_ref, 1)):
        ref[slot, 0:ATOMS, :] = jnp.where(live, src[...].astype(f32), 0.0).astype(bf16)
        ref[slot, ATOMS:PACK, :] = rows
    pl.semaphore_wait(barrier, len(peers))
    mine = plate_ref.at[p]
    out = [send_to(mine, mine, chip_send, chip_recv, d, (t, chips[d] * 2 + core)) for d in range(1, 8)]
    out.append(send_to(mine, mine, mate_send, mate_recv, 0, mate))
    up = send_to(tower_ref.at[1], tower_ref.at[0], tower_send, tower_recv, 0, above)
    down = send_to(tower_ref.at[1], tower_ref.at[2], tower_send, tower_recv, 1, below)
    passed = []
    for d in range(1, 8):
        out[d - 1].wait_recv()
        block = plate_ref.at[back[d] * 2 + core]
        passed.append(send_to(block, block, mate_send, mate_recv, d, mate))
    for copy in local[3:]:
        copy.wait()
    for copy in out:
        copy.wait_send()
    out[7].wait_recv()
    for copy in passed + [up, down]:
        copy.wait()


def gather(count, feat, adj, pos, params):
    smem = pl.BlockSpec(memory_space=pltpu.SMEM)
    vmem = pl.BlockSpec(memory_space=pltpu.VMEM)
    hbm = pl.BlockSpec(memory_space=pltpu.HBM)
    out = pl.pallas_call(
        gather_kernel,
        out_shape=[jax.ShapeDtypeStruct((BRICKS, PACK, F), bf16), jax.ShapeDtypeStruct((3, PACK, F), bf16)]
        + [jax.ShapeDtypeStruct(x.shape, x.dtype) for x in params],
        in_specs=[smem] + [hbm] * 10,
        out_specs=[vmem] * 9,
        scratch_shapes=[pltpu.VMEM((ATOMS, F), bf16), pltpu.VMEM((ATOMS, F), bf16), pltpu.VMEM((3, ATOMS), bf16), pltpu.SemaphoreType.DMA((10,))]
        + [pltpu.SemaphoreType.DMA((8,))] * 4 + [pltpu.SemaphoreType.DMA((2,))] * 2,
        compiler_params=pltpu.CompilerParams(collective_id=0, has_side_effects=True, vmem_limit_bytes=24 << 20),
        name="gather",
    )(count, feat, adj, pos, *params)
    return out[0], out[1], out[2:]


def reduce_kernel(
    pack_ref, tg_ref, gw_ref, acc_ref, w3_buf,
    mate_buf, send_buf, chip_buf, tower_buf, w1_buf, w2_own, w2_buf,
    mate_send, mate_recv, chip_send, chip_recv, tower_send, tower_recv, w_send, w_recv,
):
    t = lax.axis_index("tower")
    p = lax.axis_index("plate")
    q, core = p // 2, p % 2
    mate = (t, q * 2 + 1 - core)
    chips = [(q + d) % 8 for d in range(8)]
    plate = [(t, (p + d) % 16) for d in range(16)]
    tower = [((t + d) % 16, p) for d in range(16)]
    greet(plate[1:] + tower[1:])
    first = [send_to(gw_ref.at[(p + d) % 16], w1_buf.at[d], w_send.at[0], w_recv.at[0], d, plate[d]) for d in range(1, 16)]
    halves = [send_to(pack_ref.at[chips[d] * 2 + 1 - core], mate_buf.at[d], mate_send, mate_recv, d, mate) for d in (1, 2, 3, 4, 5, 6, 7, 0)]
    up = send_to(tg_ref.at[2], tower_buf.at[0], tower_send, tower_recv, 0, tower[1])
    down = send_to(tg_ref.at[0], tower_buf.at[1], tower_send, tower_recv, 1, tower[15])
    total = gw_ref[p]
    for d in range(1, 16):
        first[d - 1].wait_recv()
        total = total + w1_buf[d]
    w2_own[...] = total
    second = [send_to(w2_own, w2_buf.at[d], w_send.at[1], w_recv.at[1], d, tower[d]) for d in range(1, 16)]
    chip = []
    for d in range(1, 8):
        halves[d - 1].wait_recv()
        send_buf[d] = (pack_ref[chips[d] * 2 + core].astype(f32) + mate_buf[d].astype(f32)).astype(bf16)
        chip.append(send_to(send_buf.at[d], chip_buf.at[d], chip_send, chip_recv, d, (t, chips[d] * 2 + core)))
    for d in range(1, 16):
        second[d - 1].wait_recv()
        total = total + w2_buf[d]
    w3_buf[p] = total
    third = [send_to(w3_buf.at[p], w3_buf.at[p], w_send.at[2], w_recv.at[2], d, plate[d]) for d in range(1, 16)]
    halves[7].wait_recv()
    acc = pack_ref[p].astype(f32) + mate_buf[0].astype(f32)
    for d in range(1, 8):
        chip[d - 1].wait_recv()
        acc = acc + chip_buf[d].astype(f32)
    acc_ref[0:ATOMS, :] = acc[0:ATOMS]
    up.wait_recv()
    down.wait_recv()
    acc_ref[ATOMS:PACK, :] = acc[ATOMS:PACK] + tg_ref[1] + tower_buf[0] + tower_buf[1]
    for d in range(1, 16):
        third[d - 1].wait_recv()
    for copy in first + halves + [up, down] + second + chip + third:
        copy.wait_send()


def reduce(pack, tg, gw):
    vmem = pl.BlockSpec(memory_space=pltpu.VMEM)
    weights = pltpu.VMEM((16, WROWS, F), f32)
    dma = pltpu.SemaphoreType.DMA
    return pl.pallas_call(
        reduce_kernel,
        out_shape=(jax.ShapeDtypeStruct((PACK, F), f32), jax.ShapeDtypeStruct((16, WROWS, F), f32)),
        in_specs=[vmem] * 3,
        out_specs=[vmem] * 2,
        scratch_shapes=[pltpu.VMEM((8, PACK, F), bf16)] * 3 + [
            pltpu.VMEM((2, 16, F), f32), weights, pltpu.VMEM((WROWS, F), f32), weights,
            dma((8,)), dma((8,)), dma((8,)), dma((8,)), dma((2,)), dma((2,)), dma((3, 16)), dma((3, 16)),
        ],
        compiler_params=pltpu.CompilerParams(collective_id=1, has_side_effects=True, vmem_limit_bytes=24 << 20),
        name="reduce",
    )(pack, tg, gw)


def finish_kernel(cnt_s, acc_ref, w_ref, gf_out, gp_out, wr_out, br_out, wf_out, bf_out):
    gf_out[0] = jnp.where(iota((ATOMS, F), 0) < cnt_s[0, 0], acc_ref[0:ATOMS, :], 0.0)
    for k in range(2):
        for d in range(3):
            gp_out[d, :, k * F:(k + 1) * F] = acc_ref[ATOMS + 3 * k + d:ATOMS + 3 * k + d + 1, :]
    scale = lax.rsqrt(w_ref[11][0:1] * (TILE * TILE))
    wf_out[...] = w_ref[0:8].reshape(F, F) * -scale
    bf_out[...] = w_ref[8][0:1] * scale
    wr_out[...] = w_ref[9] * scale
    br_out[...] = w_ref[10][0:1] * scale


def finish(count, acc, weights):
    smem = pl.BlockSpec(memory_space=pltpu.SMEM)
    vmem = pl.BlockSpec(memory_space=pltpu.VMEM)
    return pl.pallas_call(
        finish_kernel,
        out_shape=(
            jax.ShapeDtypeStruct((1, ATOMS, F), f32), jax.ShapeDtypeStruct((3, 1, ATOMS), f32), jax.ShapeDtypeStruct((NRBF, F), f32),
            jax.ShapeDtypeStruct((1, F), f32), jax.ShapeDtypeStruct((F, F), f32), jax.ShapeDtypeStruct((1, F), f32),
        ),
        in_specs=[smem, vmem, vmem],
        out_specs=[vmem] * 6,
        compiler_params=pltpu.CompilerParams(vmem_limit_bytes=8 << 20),
        name="finish",
    )(count, acc, weights)


def local(features, adjoint, positions, w_rbf, b_rbf, w_filter, b_filter, atom_counts, tile_counts, tower_tiles, plate_tiles, image_shifts):
    params = [pltpu.with_memory_space_constraint(x, pltpu.HBM) for x in (tower_tiles, plate_tiles, image_shifts, w_rbf, b_rbf.reshape(1, F), w_filter, b_filter.reshape(1, F))]
    plate, tower, params = gather(atom_counts, *[pltpu.with_memory_space_constraint(x, pltpu.HBM) for x in (features[0], adjoint[0], positions[:, 0, :])], params)
    pack, tg, gw = pairs(tile_counts, tower, plate, params)
    gf, gp, wr, br, wf, bf = finish(atom_counts, *reduce(pack, tg, gw))
    return gf, gp, wr, br[0], wf, bf[0]


def solution(mesh):
    from jax.sharding import PartitionSpec as P
    brick = P("tower", "plate", None)
    one = P("tower", "plate")
    return jax.shard_map(
        local, mesh=mesh,
        in_specs=(brick, brick, P(None, "tower", "plate"), P(), P(), P(), P(), one, one, brick, brick, brick),
        out_specs=(brick, P(None, "tower", "plate"), P(), P(), P(), P()),
        check_vma=False,
    )
```

```python
import math

import jax
import jax.numpy as jnp
from jax import lax
from jax.experimental import pallas as pl
from jax.experimental.pallas import tpu as pltpu

F = 128
TILE = 32
PAIRS = TILE * TILE
MAXT = 56
ATOMS = 256
PACK = ATOMS + 16
BRICKS = 16
WROWS = 16
ROWS = 64
TOWER = 24
PLATE = 128
NRBF = 16
cutoff = 3.0
soften = 0.01
sharp = 10.0
f32 = jnp.float32
bf16 = jnp.bfloat16

NN = (((1,), (0,)), ((), ()))
NT = (((1,), (1,)), ((), ()))
TN = (((0,), (0,)), ((), ()))


def dot(a, b, dims=NN):
    return lax.dot_general(a, b, dims, preferred_element_type=f32)


def iota(shape, axis):
    return lax.broadcasted_iota(jnp.int32, shape, axis)


def split(x):
    hi = x.astype(bf16)
    return hi, (x - hi.astype(f32)).astype(bf16)


def sine(x):
    y = x * x
    acc = jnp.full_like(x, 1.0 / 6227020800.0)
    for c in (-1.0 / 39916800.0, 1.0 / 362880.0, -1.0 / 5040.0, 1.0 / 120.0, -1.0 / 6.0, 1.0):
        acc = acc * y + c
    return acc * x


def three(x):
    hi = x.astype(bf16).astype(f32)
    mid = (x - hi).astype(bf16).astype(f32)
    return [hi, mid, x - hi - mid]


def pairs_kernel(
    cnt_s,
    tower_ref, plate_ref, u_ref, v_ref, c_ref,
    wr_ref, br_ref, wf_ref, bf_ref,
    pack_ref, tg_ref, gw_ref,
    disp_ref, dist_ref, env_ref, tan_ref, dd_ref, rep_ref, gf_ref, list_ref, sum_ref, u_s, v_s, flag_ref, flag_s, order_s, list_sem,
    *, chunk, tiles,
):
    count = cnt_s[0, 0]
    lists_in = [pltpu.make_async_copy(u_ref, u_s, list_sem.at[0]), pltpu.make_async_copy(v_ref, v_s, list_sem.at[1])]
    for copy in lists_in:
        copy.start()
    list_ref[...] = jnp.zeros(list_ref.shape, f32)
    for k, ref in enumerate((u_ref, v_ref, c_ref)):
        list_ref[k:k + 1, 0:MAXT] = ref[0].astype(f32)
    lists = list_ref[...]
    columns = lists.T.astype(jnp.int32)
    rrow = lists[0:1, 0:ROWS].astype(jnp.int32)
    srow = lists[1:2, 0:ROWS].astype(jnp.int32)
    ucol = columns[0:ROWS, 0:1]
    vcol = columns[0:ROWS, 1:2]
    ccol = columns[0:ROWS, 2:3]
    rep = (iota((TILE, PAIRS), 1) >> 5 == iota((TILE, PAIRS), 0)).astype(bf16)
    rep_ref[...] = rep
    rep4 = (iota((F, PAIRS), 1) >> 5 == (iota((F, PAIRS), 0) & 31)).astype(bf16)
    til4 = ((iota((F, PAIRS), 1) & 31) == (iota((F, PAIRS), 0) & 31)).astype(bf16)
    group = iota((ROWS, F), 1) >> 5
    in_u = group == (ucol & 3)
    in_v = group == (vcol & 3)
    row_u = (ucol >> 3) * 16 + ((ucol >> 2) & 1) * 3
    row_v = (vcol >> 3) * 16 + ((vcol >> 2) & 1) * 3
    t_pos = tower_ref[:, ATOMS:PACK, :].reshape(48, F)
    p_pos = plate_ref[:, ATOMS:PACK, :].reshape(256, F)
    third = (ccol >= 3).astype(jnp.int32) + (ccol >= 6).astype(jnp.int32)
    shifts = (third - 1, ccol - 3 * third - 1, (ucol >> 3) - 1)
    pick_u = ((ucol >> 3) * 16 + 6 == iota((ROWS, 48), 1)).astype(bf16)
    pick_v = ((vcol >> 3) * 16 + 6 == iota((ROWS, 256), 1)).astype(bf16)
    first_u = ((ucol & 7) * TILE).astype(f32)
    first_v = ((vcol & 7) * TILE).astype(f32)
    live = (first_u < dot(pick_u, t_pos)) & (first_v < dot(pick_v, p_pos)) & (iota((ROWS, F), 0) < count)
    flag_ref[...] = live.astype(f32).T[0:8].astype(jnp.int32)
    flags = pltpu.make_async_copy(flag_ref, flag_s, list_sem.at[2])
    flags.start()
    square = jnp.zeros((ROWS, PAIRS), f32)
    for d in range(3):
        pick_u = (row_u + d == iota((ROWS, 48), 1)).astype(bf16)
        pick_v = (row_v + d == iota((ROWS, 256), 1)).astype(bf16)
        recv = jnp.where(in_u, dot(pick_u, t_pos), 0.0)
        send = jnp.where(in_v, dot(pick_v, p_pos), 0.0)
        disp = dot(recv.astype(bf16), rep4) - dot(send.astype(bf16), til4) + shifts[d].astype(f32)
        disp_ref[d] = disp
        square = square + disp * disp
    dist = jnp.sqrt(square + soften)
    dist_ref[...] = dist
    inside = (dist < cutoff) & (iota((ROWS, PAIRS), 0) < count)
    theta = jnp.minimum(dist, cutoff) * (math.pi / (2 * cutoff))
    cosine = jnp.maximum(sine(math.pi / 2 - theta), 1e-6)
    env_ref[...] = jnp.where(inside, cosine * cosine, 0.0)
    tan_ref[...] = jnp.where(inside, (-math.pi / cutoff) * sine(theta) / cosine, 0.0)
    dd_ref[...] = jnp.zeros((ROWS, PAIRS), f32)
    gf_ref[...] = jnp.zeros(gf_ref.shape, f32)
    sum_ref[...] = jnp.zeros(sum_ref.shape, f32)

    centres = iota((NRBF, 1), 0).astype(f32) * (cutoff / (NRBF - 1))
    ones = jnp.ones((NRBF, chunk), bf16)
    wr = wr_ref[...]
    zeros = jnp.zeros((NRBF - 3, F), f32)
    w1 = jnp.concatenate([wr.astype(f32) * 0.5] + three(br_ref[...] * 0.5) + [zeros], axis=0).T.astype(bf16)
    wf = wf_ref[...].astype(f32)
    nwft = jnp.concatenate([-wf.T, jnp.concatenate(three(bf_ref[...]) + [zeros], axis=0).T], axis=1).astype(bf16)
    hwf = (wf * 0.5).astype(bf16)
    fold = ((iota((TILE, 2 * F), 1) & 31) == iota((TILE, 2 * F), 0)).astype(bf16)

    def body(step, carry):
        entries = [order_s[step * tiles + k] for k in range(tiles)]
        streams = []
        for e in entries:
            listed = jnp.minimum(e, MAXT - 1)
            u = u_s[0, 0, listed]
            v = v_s[0, 0, listed]
            adj = tower_ref[u >> 3, pl.ds(pl.multiple_of((u & 7) * TILE, TILE), TILE), :]
            adj = jnp.concatenate([adj] * 2, axis=0)
            feat = plate_ref[v >> 3, pl.ds(pl.multiple_of((v & 7) * TILE, TILE), TILE), :].astype(f32)
            feat4 = jnp.concatenate([feat] * 4, axis=0).T
            wide = jnp.concatenate([feat4] * (chunk // F), axis=1)
            for s in range(0, PAIRS, chunk):
                streams.append(dict(e=e, v=v, adj=adj, wide=wide, lanes=pl.ds(s, chunk)))
        for x in streams:
            x['off'] = dist_ref[pl.ds(x['e'], 1), x['lanes']] - centres
            x['basis'] = jnp.exp(-sharp * x['off'] * x['off'])
            x['inputs'] = jnp.concatenate([x['basis'].astype(bf16), ones], axis=0)
            x['half'] = dot(w1, x['inputs'])
            hi, lo = split(env_ref[pl.ds(x['e'], 1), x['lanes']])
            member = rep_ref[:, x['lanes']]
            spread = jnp.concatenate([member * hi, member * lo], axis=0)
            x['adj_env'] = dot(x['adj'], spread, TN)
        for x in streams:
            x['t'] = jnp.tanh(x['half'])
            x['soft_b'] = jnp.concatenate([jnp.log(1.0 - x['t']).astype(bf16), ones], axis=0)
            x['d_raw_b'] = (x['adj_env'] * x['wide']).astype(bf16)
        for x in streams:
            x['filt'] = dot(nwft, x['soft_b'])
            x['d_soft'] = dot(hwf, x['d_raw_b'])
        for x in streams:
            x['d_pre_b'] = (x['d_soft'] * (1.0 + x['t'])).astype(bf16)
            x['y'] = x['adj_env'] * x['filt']
            x['zsum'] = jnp.sum(x['y'] * x['wide'], axis=0, keepdims=True)
        gw = jnp.zeros((2 * F, F + 2 * NRBF), f32)
        for x in streams:
            d_basis = dot(wr, x['d_pre_b'])
            d_dist = jnp.sum(d_basis * x['basis'] * x['off'], axis=0, keepdims=True) * (-2.0 * sharp)
            x['dd'] = d_dist + tan_ref[pl.ds(x['e'], 1), x['lanes']] * x['zsum']
            grads = jnp.concatenate([x['d_raw_b'], x['d_pre_b']], axis=0)
            values = jnp.concatenate([x['soft_b'], x['inputs'][0:NRBF]], axis=0)
            gw = gw + dot(grads, values, NT)
        for e in entries:
            acc = jnp.zeros((F, F), f32)
            for x in streams:
                if x['e'] is e:
                    v = x['v']
                    dd_ref[pl.ds(e, 1), x['lanes']] = x['dd']
                    for q in range(0, chunk, F):
                        acc = acc + x['y'][:, q:q + F]
            gf_ref[v] += dot(fold, jnp.concatenate(split(acc), axis=1), NT)
        sum_ref[...] += gw
        return carry

    for copy in lists_in:
        copy.wait()
    flags.wait()

    def keep(e, n):
        order_s[n] = e
        return n + flag_s[0, e]

    kept = lax.fori_loop(0, MAXT, keep, 0)
    for k in range(tiles - 1):
        order_s[kept + k] = ROWS - 1
    lax.fori_loop(0, (kept + tiles - 1) // tiles, body, 0)

    radial = dd_ref[...] / dist_ref[...]
    t_sum = jnp.zeros((48, F), f32)
    p_sum = jnp.zeros((256, F), f32)
    to_u = (rrow >> 3) * 16 + ((rrow >> 2) & 1) * 3
    to_v = (srow >> 3) * 16 + ((srow >> 2) & 1) * 3
    pulls = jnp.concatenate([part for d in range(3) for part in split(disp_ref[d] * radial)], axis=0)
    recv_all = dot(pulls, rep4, NT)
    send_all = dot(pulls, til4, NT)
    for d in range(3):
        at = 2 * ROWS * d
        recv_hi, recv_lo = split(jnp.where(in_u, recv_all[at:at + ROWS] + recv_all[at + ROWS:at + 2 * ROWS], 0.0))
        send_hi, send_lo = split(jnp.where(in_v, send_all[at:at + ROWS] + send_all[at + ROWS:at + 2 * ROWS], 0.0))
        put_u = (to_u + d == iota((48, ROWS), 0)).astype(bf16)
        put_v = (to_v + d == iota((256, ROWS), 0)).astype(bf16)
        t_sum = t_sum + dot(put_u, recv_hi) + dot(put_u, recv_lo)
        p_sum = p_sum - dot(put_v, send_hi) - dot(put_v, send_lo)
    tg_ref[...] = t_sum.reshape(3, 16, F)
    pack_ref[:, ATOMS:PACK, :] = p_sum.astype(bf16).reshape(BRICKS, 16, F)
    pack_ref[:, 0:ATOMS, :] = gf_ref[...].reshape(BRICKS, ATOMS, F).astype(bf16)
    gw_ref[0:8] = sum_ref[0:F, 0:F].T.reshape(8, WROWS, F)
    gw_ref[8] = sum_ref[0:F, F:F + 2 * NRBF].T[0:WROWS]
    rest = sum_ref[F:2 * F, F:F + 2 * NRBF].T
    gw_ref[9] = rest[NRBF:2 * NRBF]
    gw_ref[10] = rest[0:NRBF]
    gw_ref[12:16] = jnp.zeros((4, WROWS, F), f32)
    gw_ref[11] = jnp.full((WROWS, F), count, jnp.int32).astype(f32)


def pairs(count, tower, plate, params, chunk=256, tiles=2):
    smem = pl.BlockSpec(memory_space=pltpu.SMEM)
    vmem = pl.BlockSpec(memory_space=pltpu.VMEM)
    return pl.pallas_call(
        lambda *refs: pairs_kernel(*refs, chunk=chunk, tiles=tiles),
        out_shape=(
            jax.ShapeDtypeStruct((BRICKS, PACK, F), bf16),
            jax.ShapeDtypeStruct((3, 16, F), f32),
            jax.ShapeDtypeStruct((16, WROWS, F), f32),
        ),
        in_specs=[smem] + [vmem] * 9,
        out_specs=[vmem] * 3,
        scratch_shapes=[
            pltpu.VMEM((3, ROWS, PAIRS), f32),
            pltpu.VMEM((ROWS, PAIRS), f32),
            pltpu.VMEM((ROWS, PAIRS), f32),
            pltpu.VMEM((ROWS, PAIRS), f32),
            pltpu.VMEM((ROWS, PAIRS), f32),
            pltpu.VMEM((TILE, PAIRS), bf16),
            pltpu.VMEM((PLATE, TILE, F), f32),
            pltpu.VMEM((8, F), f32),
            pltpu.VMEM((2 * F, F + 2 * NRBF), f32),
            pltpu.SMEM((1, 1, MAXT), jnp.int32),
            pltpu.SMEM((1, 1, MAXT), jnp.int32),
            pltpu.VMEM((8, ROWS), jnp.int32),
            pltpu.SMEM((8, ROWS), jnp.int32),
            pltpu.SMEM((ROWS,), jnp.int32),
            pltpu.SemaphoreType.DMA((3,)),
        ],
        compiler_params=pltpu.CompilerParams(vmem_limit_bytes=48 << 20),
        name="pairs",
    )(count, tower, plate, *params)


def send_to(src, dst, sends, recvs, slot, device):
    copy = pltpu.make_async_remote_copy(
        src_ref=src, dst_ref=dst, send_sem=sends.at[slot], recv_sem=recvs.at[slot],
        device_id=device, device_id_type=pl.DeviceIdType.MESH,
    )
    copy.start()
    return copy


def greet(devices):
    barrier = pltpu.get_barrier_semaphore()
    for device in devices:
        pl.semaphore_signal(barrier, inc=1, device_id=device, device_id_type=pl.DeviceIdType.MESH)
    pl.semaphore_wait(barrier, len(devices))


def gather_kernel(
    cnt_s, feat_hbm, adj_hbm, pos_hbm, *refs,
):
    params_hbm, (plate_ref, tower_ref), params = refs[:7], refs[7:9], refs[9:16]
    feat_ref, adj_ref, pos_ref, local_sem, chip_send, chip_recv, mate_send, mate_recv, tower_send, tower_recv = refs[16:]
    t = lax.axis_index("tower")
    p = lax.axis_index("plate")
    q, core = p // 2, p % 2
    mate = (t, q * 2 + 1 - core)
    above = ((t + 1) % 16, p)
    below = ((t + 15) % 16, p)
    chips = [(q + d) % 8 for d in range(8)]
    back = [(q + 8 - d) % 8 for d in range(8)]
    local = []
    for k, (src, dst) in enumerate(zip((feat_hbm, adj_hbm, pos_hbm) + params_hbm, (feat_ref, adj_ref, pos_ref) + params)):
        local.append(pltpu.make_async_copy(src, dst, local_sem.at[k]))
        local[k].start()
    barrier = pltpu.get_barrier_semaphore()
    peers = [(t, chips[d] * 2 + core) for d in range(1, 8)] + [mate, above, below]
    for device in peers:
        pl.semaphore_signal(barrier, inc=1, device_id=device, device_id_type=pl.DeviceIdType.MESH)
    local[0].wait()
    local[1].wait()
    local[2].wait()
    live = iota((ATOMS, F), 0) < cnt_s[0, 0]
    halves = [pos_ref[:, k * F:(k + 1) * F].astype(f32) for k in range(2)]
    atoms = jnp.full((1, F), cnt_s[0, 0], jnp.int32).astype(f32)
    rows = jnp.concatenate(halves + [atoms, jnp.zeros((9, F), f32)], axis=0).astype(bf16)
    for src, ref, slot in ((feat_ref, plate_ref, p), (adj_ref, tower_ref, 1)):
        ref[slot, 0:ATOMS, :] = jnp.where(live, src[...].astype(f32), 0.0).astype(bf16)
        ref[slot, ATOMS:PACK, :] = rows
    pl.semaphore_wait(barrier, len(peers))
    mine = plate_ref.at[p]
    out = [send_to(mine, mine, chip_send, chip_recv, d, (t, chips[d] * 2 + core)) for d in range(1, 8)]
    out.append(send_to(mine, mine, mate_send, mate_recv, 0, mate))
    up = send_to(tower_ref.at[1], tower_ref.at[0], tower_send, tower_recv, 0, above)
    down = send_to(tower_ref.at[1], tower_ref.at[2], tower_send, tower_recv, 1, below)
    passed = []
    for d in range(1, 8):
        out[d - 1].wait_recv()
        block = plate_ref.at[back[d] * 2 + core]
        passed.append(send_to(block, block, mate_send, mate_recv, d, mate))
    for copy in local[3:]:
        copy.wait()
    for copy in out:
        copy.wait_send()
    out[7].wait_recv()
    for copy in passed + [up, down]:
        copy.wait()


def gather(count, feat, adj, pos, params):
    smem = pl.BlockSpec(memory_space=pltpu.SMEM)
    vmem = pl.BlockSpec(memory_space=pltpu.VMEM)
    hbm = pl.BlockSpec(memory_space=pltpu.HBM)
    out = pl.pallas_call(
        gather_kernel,
        out_shape=[jax.ShapeDtypeStruct((BRICKS, PACK, F), bf16), jax.ShapeDtypeStruct((3, PACK, F), bf16)]
        + [jax.ShapeDtypeStruct(x.shape, x.dtype) for x in params],
        in_specs=[smem] + [hbm] * 10,
        out_specs=[vmem] * 9,
        scratch_shapes=[pltpu.VMEM((ATOMS, F), bf16), pltpu.VMEM((ATOMS, F), bf16), pltpu.VMEM((3, ATOMS), bf16), pltpu.SemaphoreType.DMA((10,))]
        + [pltpu.SemaphoreType.DMA((8,))] * 4 + [pltpu.SemaphoreType.DMA((2,))] * 2,
        compiler_params=pltpu.CompilerParams(collective_id=0, has_side_effects=True, vmem_limit_bytes=24 << 20),
        name="gather",
    )(count, feat, adj, pos, *params)
    return out[0], out[1], out[2:]


def reduce_kernel(
    pack_ref, tg_ref, gw_ref, acc_ref, w3_buf,
    mate_buf, send_buf, chip_buf, tower_buf, w1_buf, w2_own, w2_buf,
    mate_send, mate_recv, chip_send, chip_recv, tower_send, tower_recv, w_send, w_recv,
):
    t = lax.axis_index("tower")
    p = lax.axis_index("plate")
    q, core = p // 2, p % 2
    mate = (t, q * 2 + 1 - core)
    chips = [(q + d) % 8 for d in range(8)]
    plate = [(t, (p + d) % 16) for d in range(16)]
    tower = [((t + d) % 16, p) for d in range(16)]
    greet(plate[1:] + tower[1:])
    first = [send_to(gw_ref.at[(p + d) % 16], w1_buf.at[d], w_send.at[0], w_recv.at[0], d, plate[d]) for d in range(1, 16)]
    halves = [send_to(pack_ref.at[chips[d] * 2 + 1 - core], mate_buf.at[d], mate_send, mate_recv, d, mate) for d in (1, 2, 3, 4, 5, 6, 7, 0)]
    up = send_to(tg_ref.at[2], tower_buf.at[0], tower_send, tower_recv, 0, tower[1])
    down = send_to(tg_ref.at[0], tower_buf.at[1], tower_send, tower_recv, 1, tower[15])
    total = gw_ref[p]
    for d in range(1, 16):
        first[d - 1].wait_recv()
        total = total + w1_buf[d]
    w2_own[...] = total
    second = [send_to(w2_own, w2_buf.at[d], w_send.at[1], w_recv.at[1], d, tower[d]) for d in range(1, 16)]
    chip = []
    for d in range(1, 8):
        halves[d - 1].wait_recv()
        send_buf[d] = (pack_ref[chips[d] * 2 + core].astype(f32) + mate_buf[d].astype(f32)).astype(bf16)
        chip.append(send_to(send_buf.at[d], chip_buf.at[d], chip_send, chip_recv, d, (t, chips[d] * 2 + core)))
    for d in range(1, 16):
        second[d - 1].wait_recv()
        total = total + w2_buf[d]
    w3_buf[p] = total
    third = [send_to(w3_buf.at[p], w3_buf.at[p], w_send.at[2], w_recv.at[2], d, plate[d]) for d in range(1, 16)]
    halves[7].wait_recv()
    acc = pack_ref[p].astype(f32) + mate_buf[0].astype(f32)
    for d in range(1, 8):
        chip[d - 1].wait_recv()
        acc = acc + chip_buf[d].astype(f32)
    acc_ref[0:ATOMS, :] = acc[0:ATOMS]
    up.wait_recv()
    down.wait_recv()
    acc_ref[ATOMS:PACK, :] = acc[ATOMS:PACK] + tg_ref[1] + tower_buf[0] + tower_buf[1]
    for d in range(1, 16):
        third[d - 1].wait_recv()
    for copy in first + halves + [up, down] + second + chip + third:
        copy.wait_send()


def reduce(pack, tg, gw):
    vmem = pl.BlockSpec(memory_space=pltpu.VMEM)
    weights = pltpu.VMEM((16, WROWS, F), f32)
    dma = pltpu.SemaphoreType.DMA
    return pl.pallas_call(
        reduce_kernel,
        out_shape=(jax.ShapeDtypeStruct((PACK, F), f32), jax.ShapeDtypeStruct((16, WROWS, F), f32)),
        in_specs=[vmem] * 3,
        out_specs=[vmem] * 2,
        scratch_shapes=[pltpu.VMEM((8, PACK, F), bf16)] * 3 + [
            pltpu.VMEM((2, 16, F), f32), weights, pltpu.VMEM((WROWS, F), f32), weights,
            dma((8,)), dma((8,)), dma((8,)), dma((8,)), dma((2,)), dma((2,)), dma((3, 16)), dma((3, 16)),
        ],
        compiler_params=pltpu.CompilerParams(collective_id=1, has_side_effects=True, vmem_limit_bytes=24 << 20),
        name="reduce",
    )(pack, tg, gw)


def finish_kernel(cnt_s, acc_ref, w_ref, gf_out, gp_out, wr_out, br_out, wf_out, bf_out):
    gf_out[0] = jnp.where(iota((ATOMS, F), 0) < cnt_s[0, 0], acc_ref[0:ATOMS, :], 0.0)
    for k in range(2):
        for d in range(3):
            gp_out[d, :, k * F:(k + 1) * F] = acc_ref[ATOMS + 3 * k + d:ATOMS + 3 * k + d + 1, :]
    scale = lax.rsqrt(w_ref[11][0:1] * (TILE * TILE))
    wf_out[...] = w_ref[0:8].reshape(F, F) * -scale
    bf_out[...] = w_ref[8][0:1] * scale
    wr_out[...] = w_ref[9] * scale
    br_out[...] = w_ref[10][0:1] * scale


def finish(count, acc, weights):
    smem = pl.BlockSpec(memory_space=pltpu.SMEM)
    vmem = pl.BlockSpec(memory_space=pltpu.VMEM)
    return pl.pallas_call(
        finish_kernel,
        out_shape=(
            jax.ShapeDtypeStruct((1, ATOMS, F), f32), jax.ShapeDtypeStruct((3, 1, ATOMS), f32), jax.ShapeDtypeStruct((NRBF, F), f32),
            jax.ShapeDtypeStruct((1, F), f32), jax.ShapeDtypeStruct((F, F), f32), jax.ShapeDtypeStruct((1, F), f32),
        ),
        in_specs=[smem, vmem, vmem],
        out_specs=[vmem] * 6,
        compiler_params=pltpu.CompilerParams(vmem_limit_bytes=8 << 20),
        name="finish",
    )(count, acc, weights)


def local(features, adjoint, positions, w_rbf, b_rbf, w_filter, b_filter, atom_counts, tile_counts, tower_tiles, plate_tiles, image_shifts):
    params = [pltpu.with_memory_space_constraint(x, pltpu.HBM) for x in (tower_tiles, plate_tiles, image_shifts, w_rbf, b_rbf.reshape(1, F), w_filter, b_filter.reshape(1, F))]
    plate, tower, params = gather(atom_counts, *[pltpu.with_memory_space_constraint(x, pltpu.HBM) for x in (features[0], adjoint[0], positions[:, 0, :])], params)
    pack, tg, gw = pairs(tile_counts, tower, plate, params)
    gf, gp, wr, br, wf, bf = finish(atom_counts, *reduce(pack, tg, gw))
    return gf, gp, wr, br[0], wf, bf[0]


def solution(mesh):
    from jax.sharding import PartitionSpec as P
    brick = P("tower", "plate", None)
    one = P("tower", "plate")
    return jax.shard_map(
        local, mesh=mesh,
        in_specs=(brick, brick, P(None, "tower", "plate"), P(), P(), P(), P(), one, one, brick, brick, brick),
        out_specs=(brick, P(None, "tower", "plate"), P(), P(), P(), P()),
        check_vma=False,
    )
```

```python
import math

import jax
import jax.numpy as jnp
from jax import lax
from jax.experimental import pallas as pl
from jax.experimental.pallas import tpu as pltpu

F = 128
TILE = 32
PAIRS = TILE * TILE
MAXT = 56
ATOMS = 256
PACK = ATOMS + 16
BRICKS = 16
WROWS = 16
ROWS = 64
TOWER = 24
PLATE = 128
NRBF = 16
cutoff = 3.0
soften = 0.01
sharp = 10.0
f32 = jnp.float32
bf16 = jnp.bfloat16

NN = (((1,), (0,)), ((), ()))
NT = (((1,), (1,)), ((), ()))
TN = (((0,), (0,)), ((), ()))


def dot(a, b, dims=NN):
    return lax.dot_general(a, b, dims, preferred_element_type=f32)


def iota(shape, axis):
    return lax.broadcasted_iota(jnp.int32, shape, axis)


def split(x):
    hi = x.astype(bf16)
    return hi, (x - hi.astype(f32)).astype(bf16)


def sine(x):
    y = x * x
    acc = jnp.full_like(x, 1.0 / 6227020800.0)
    for c in (-1.0 / 39916800.0, 1.0 / 362880.0, -1.0 / 5040.0, 1.0 / 120.0, -1.0 / 6.0, 1.0):
        acc = acc * y + c
    return acc * x


def three(x):
    hi = x.astype(bf16).astype(f32)
    mid = (x - hi).astype(bf16).astype(f32)
    return [hi, mid, x - hi - mid]


def pairs_kernel(
    cnt_s,
    tower_ref, plate_ref, u_ref, v_ref, c_ref,
    wr_ref, br_ref, wf_ref, bf_ref,
    gf_ref, sum_ref, disp_ref, dist_ref, dd_ref, list_ref,
    env_ref, tan_ref, rep_ref, u_s, v_s, flag_ref, flag_s, order_s, list_sem,
    *, chunk, tiles,
):
    count = cnt_s[0, 0]
    lists_in = [pltpu.make_async_copy(u_ref, u_s, list_sem.at[0]), pltpu.make_async_copy(v_ref, v_s, list_sem.at[1])]
    for copy in lists_in:
        copy.start()
    list_ref[...] = jnp.zeros(list_ref.shape, f32)
    for k, ref in enumerate((u_ref, v_ref, c_ref)):
        list_ref[k:k + 1, 0:MAXT] = ref[0].astype(f32)
    lists = list_ref[...]
    columns = lists.T.astype(jnp.int32)
    ucol = columns[0:ROWS, 0:1]
    vcol = columns[0:ROWS, 1:2]
    ccol = columns[0:ROWS, 2:3]
    rep = (iota((TILE, PAIRS), 1) >> 5 == iota((TILE, PAIRS), 0)).astype(bf16)
    rep_ref[...] = rep
    rep4 = (iota((F, PAIRS), 1) >> 5 == (iota((F, PAIRS), 0) & 31)).astype(bf16)
    til4 = ((iota((F, PAIRS), 1) & 31) == (iota((F, PAIRS), 0) & 31)).astype(bf16)
    group = iota((ROWS, F), 1) >> 5
    in_u = group == (ucol & 3)
    in_v = group == (vcol & 3)
    row_u = (ucol >> 3) * 16 + ((ucol >> 2) & 1) * 3
    row_v = (vcol >> 3) * 16 + ((vcol >> 2) & 1) * 3
    t_pos = tower_ref[:, ATOMS:PACK, :].reshape(48, F)
    p_pos = plate_ref[:, ATOMS:PACK, :].reshape(256, F)
    third = (ccol >= 3).astype(jnp.int32) + (ccol >= 6).astype(jnp.int32)
    shifts = (third - 1, ccol - 3 * third - 1, (ucol >> 3) - 1)
    pick_u = ((ucol >> 3) * 16 + 6 == iota((ROWS, 48), 1)).astype(bf16)
    pick_v = ((vcol >> 3) * 16 + 6 == iota((ROWS, 256), 1)).astype(bf16)
    first_u = ((ucol & 7) * TILE).astype(f32)
    first_v = ((vcol & 7) * TILE).astype(f32)
    live = (first_u < dot(pick_u, t_pos)) & (first_v < dot(pick_v, p_pos)) & (iota((ROWS, F), 0) < count)
    flag_ref[...] = live.astype(f32).T[0:8].astype(jnp.int32)
    flags = pltpu.make_async_copy(flag_ref, flag_s, list_sem.at[2])
    flags.start()
    square = jnp.zeros((ROWS, PAIRS), f32)
    for d in range(3):
        pick_u = (row_u + d == iota((ROWS, 48), 1)).astype(bf16)
        pick_v = (row_v + d == iota((ROWS, 256), 1)).astype(bf16)
        recv = jnp.where(in_u, dot(pick_u, t_pos), 0.0)
        send = jnp.where(in_v, dot(pick_v, p_pos), 0.0)
        disp = dot(recv.astype(bf16), rep4) - dot(send.astype(bf16), til4) + shifts[d].astype(f32)
        disp_ref[d] = disp
        square = square + disp * disp
    dist = jnp.sqrt(square + soften)
    dist_ref[...] = dist
    inside = (dist < cutoff) & (iota((ROWS, PAIRS), 0) < count)
    theta = jnp.minimum(dist, cutoff) * (math.pi / (2 * cutoff))
    cosine = jnp.maximum(sine(math.pi / 2 - theta), 1e-6)
    env_ref[...] = jnp.where(inside, cosine * cosine, 0.0)
    tan_ref[...] = jnp.where(inside, (-math.pi / cutoff) * sine(theta) / cosine, 0.0)
    dd_ref[...] = jnp.zeros((ROWS, PAIRS), f32)
    gf_ref[...] = jnp.zeros(gf_ref.shape, f32)
    sum_ref[...] = jnp.zeros(sum_ref.shape, f32)

    centres = iota((NRBF, 1), 0).astype(f32) * (cutoff / (NRBF - 1))
    ones = jnp.ones((NRBF, chunk), bf16)
    wr = wr_ref[...]
    zeros = jnp.zeros((NRBF - 3, F), f32)
    w1 = jnp.concatenate([wr.astype(f32) * 0.5] + three(br_ref[...] * 0.5) + [zeros], axis=0).T.astype(bf16)
    wf = wf_ref[...].astype(f32)
    nwft = jnp.concatenate([-wf.T, jnp.concatenate(three(bf_ref[...]) + [zeros], axis=0).T], axis=1).astype(bf16)
    hwf = (wf * 0.5).astype(bf16)
    fold = ((iota((TILE, 2 * F), 1) & 31) == iota((TILE, 2 * F), 0)).astype(bf16)

    def body(step, carry):
        entries = [order_s[step * tiles + k] for k in range(tiles)]
        streams = []
        for e in entries:
            listed = jnp.minimum(e, MAXT - 1)
            u = u_s[0, 0, listed]
            v = v_s[0, 0, listed]
            adj = tower_ref[u >> 3, pl.ds(pl.multiple_of((u & 7) * TILE, TILE), TILE), :]
            adj = jnp.concatenate([adj] * 2, axis=0)
            feat = plate_ref[v >> 3, pl.ds(pl.multiple_of((v & 7) * TILE, TILE), TILE), :].astype(f32)
            feat4 = jnp.concatenate([feat] * 4, axis=0).T
            wide = jnp.concatenate([feat4] * (chunk // F), axis=1)
            for s in range(0, PAIRS, chunk):
                streams.append(dict(e=e, v=v, adj=adj, wide=wide, lanes=pl.ds(s, chunk)))
        for x in streams:
            x['off'] = dist_ref[pl.ds(x['e'], 1), x['lanes']] - centres
            x['basis'] = jnp.exp(-sharp * x['off'] * x['off'])
            x['inputs'] = jnp.concatenate([x['basis'].astype(bf16), ones], axis=0)
            x['half'] = dot(w1, x['inputs'])
            hi, lo = split(env_ref[pl.ds(x['e'], 1), x['lanes']])
            member = rep_ref[:, x['lanes']]
            spread = jnp.concatenate([member * hi, member * lo], axis=0)
            x['adj_env'] = dot(x['adj'], spread, TN)
        for x in streams:
            x['t'] = jnp.tanh(x['half'])
            x['soft_b'] = jnp.concatenate([jnp.log(1.0 - x['t']).astype(bf16), ones], axis=0)
            x['d_raw_b'] = (x['adj_env'] * x['wide']).astype(bf16)
        for x in streams:
            x['filt'] = dot(nwft, x['soft_b'])
            x['d_soft'] = dot(hwf, x['d_raw_b'])
        for x in streams:
            x['d_pre_b'] = (x['d_soft'] * (1.0 + x['t'])).astype(bf16)
            x['y'] = x['adj_env'] * x['filt']
            x['zsum'] = jnp.sum(x['y'] * x['wide'], axis=0, keepdims=True)
        gw = jnp.zeros((2 * F, F + 2 * NRBF), f32)
        for x in streams:
            d_basis = dot(wr, x['d_pre_b'])
            d_dist = jnp.sum(d_basis * x['basis'] * x['off'], axis=0, keepdims=True) * (-2.0 * sharp)
            x['dd'] = d_dist + tan_ref[pl.ds(x['e'], 1), x['lanes']] * x['zsum']
            grads = jnp.concatenate([x['d_raw_b'], x['d_pre_b']], axis=0)
            values = jnp.concatenate([x['soft_b'], x['inputs'][0:NRBF]], axis=0)
            gw = gw + dot(grads, values, NT)
        for e in entries:
            acc = jnp.zeros((F, F), f32)
            for x in streams:
                if x['e'] is e:
                    v = x['v']
                    dd_ref[pl.ds(e, 1), x['lanes']] = x['dd']
                    for q in range(0, chunk, F):
                        acc = acc + x['y'][:, q:q + F]
            gf_ref[v] += dot(fold, jnp.concatenate(split(acc), axis=1), NT)
        sum_ref[...] += gw
        return carry

    for copy in lists_in:
        copy.wait()
    flags.wait()

    def keep(e, n):
        order_s[n] = e
        return n + flag_s[0, e]

    kept = lax.fori_loop(0, MAXT, keep, 0)
    for k in range(tiles - 1):
        order_s[kept + k] = ROWS - 1
    lax.fori_loop(0, (kept + tiles - 1) // tiles, body, 0)


def pairs(count, tower, plate, params, chunk=256, tiles=2):
    smem = pl.BlockSpec(memory_space=pltpu.SMEM)
    vmem = pl.BlockSpec(memory_space=pltpu.VMEM)
    return pl.pallas_call(
        lambda *refs: pairs_kernel(*refs, chunk=chunk, tiles=tiles),
        out_shape=(
            jax.ShapeDtypeStruct((PLATE, TILE, F), f32),
            jax.ShapeDtypeStruct((2 * F, F + 2 * NRBF), f32),
            jax.ShapeDtypeStruct((3, ROWS, PAIRS), f32),
            jax.ShapeDtypeStruct((ROWS, PAIRS), f32),
            jax.ShapeDtypeStruct((ROWS, PAIRS), f32),
            jax.ShapeDtypeStruct((8, F), f32),
        ),
        in_specs=[smem] + [vmem] * 9,
        out_specs=[vmem] * 6,
        scratch_shapes=[
            pltpu.VMEM((ROWS, PAIRS), f32),
            pltpu.VMEM((ROWS, PAIRS), f32),
            pltpu.VMEM((TILE, PAIRS), bf16),
            pltpu.SMEM((1, 1, MAXT), jnp.int32),
            pltpu.SMEM((1, 1, MAXT), jnp.int32),
            pltpu.VMEM((8, ROWS), jnp.int32),
            pltpu.SMEM((8, ROWS), jnp.int32),
            pltpu.SMEM((ROWS,), jnp.int32),
            pltpu.SemaphoreType.DMA((3,)),
        ],
        compiler_params=pltpu.CompilerParams(vmem_limit_bytes=48 << 20),
        name="pairs",
    )(count, tower, plate, *params)


def send_to(src, dst, sends, recvs, slot, device):
    copy = pltpu.make_async_remote_copy(
        src_ref=src, dst_ref=dst, send_sem=sends.at[slot], recv_sem=recvs.at[slot],
        device_id=device, device_id_type=pl.DeviceIdType.MESH,
    )
    copy.start()
    return copy


def gather_kernel(
    cnt_s, feat_hbm, adj_hbm, pos_hbm, *refs,
):
    params_hbm, (plate_ref, tower_ref), params = refs[:7], refs[7:9], refs[9:16]
    feat_ref, adj_ref, pos_ref, local_sem, chip_send, chip_recv, mate_send, mate_recv, tower_send, tower_recv = refs[16:]
    t = lax.axis_index("tower")
    p = lax.axis_index("plate")
    q, core = p // 2, p % 2
    mate = (t, q * 2 + 1 - core)
    above = ((t + 1) % 16, p)
    below = ((t + 15) % 16, p)
    chips = [(q + d) % 8 for d in range(8)]
    back = [(q + 8 - d) % 8 for d in range(8)]
    local = []
    for k, (src, dst) in enumerate(zip((feat_hbm, adj_hbm, pos_hbm) + params_hbm, (feat_ref, adj_ref, pos_ref) + params)):
        local.append(pltpu.make_async_copy(src, dst, local_sem.at[k]))
        local[k].start()
    barrier = pltpu.get_barrier_semaphore()
    peers = [(t, chips[d] * 2 + core) for d in range(1, 8)] + [mate, above, below]
    for device in peers:
        pl.semaphore_signal(barrier, inc=1, device_id=device, device_id_type=pl.DeviceIdType.MESH)
    local[0].wait()
    local[1].wait()
    local[2].wait()
    live = iota((ATOMS, F), 0) < cnt_s[0, 0]
    halves = [pos_ref[:, k * F:(k + 1) * F].astype(f32) for k in range(2)]
    atoms = jnp.full((1, F), cnt_s[0, 0], jnp.int32).astype(f32)
    rows = jnp.concatenate(halves + [atoms, jnp.zeros((9, F), f32)], axis=0).astype(bf16)
    for src, ref, slot in ((feat_ref, plate_ref, p), (adj_ref, tower_ref, 1)):
        ref[slot, 0:ATOMS, :] = jnp.where(live, src[...].astype(f32), 0.0).astype(bf16)
        ref[slot, ATOMS:PACK, :] = rows
    pl.semaphore_wait(barrier, len(peers))
    mine = plate_ref.at[p]
    out = [send_to(mine, mine, chip_send, chip_recv, d, (t, chips[d] * 2 + core)) for d in range(1, 8)]
    out.append(send_to(mine, mine, mate_send, mate_recv, 0, mate))
    up = send_to(tower_ref.at[1], tower_ref.at[0], tower_send, tower_recv, 0, above)
    down = send_to(tower_ref.at[1], tower_ref.at[2], tower_send, tower_recv, 1, below)
    passed = []
    for d in range(1, 8):
        out[d - 1].wait_recv()
        block = plate_ref.at[back[d] * 2 + core]
        passed.append(send_to(block, block, mate_send, mate_recv, d, mate))
    for copy in local[3:]:
        copy.wait()
    for copy in out:
        copy.wait_send()
    out[7].wait_recv()
    for copy in passed + [up, down]:
        copy.wait()


def gather(count, feat, adj, pos, params):
    smem = pl.BlockSpec(memory_space=pltpu.SMEM)
    vmem = pl.BlockSpec(memory_space=pltpu.VMEM)
    hbm = pl.BlockSpec(memory_space=pltpu.HBM)
    out = pl.pallas_call(
        gather_kernel,
        out_shape=[jax.ShapeDtypeStruct((BRICKS, PACK, F), bf16), jax.ShapeDtypeStruct((3, PACK, F), bf16)]
        + [jax.ShapeDtypeStruct(x.shape, x.dtype) for x in params],
        in_specs=[smem] + [hbm] * 10,
        out_specs=[vmem] * 9,
        scratch_shapes=[pltpu.VMEM((ATOMS, F), bf16), pltpu.VMEM((ATOMS, F), bf16), pltpu.VMEM((3, ATOMS), bf16), pltpu.SemaphoreType.DMA((10,))]
        + [pltpu.SemaphoreType.DMA((8,))] * 4 + [pltpu.SemaphoreType.DMA((2,))] * 2,
        compiler_params=pltpu.CompilerParams(collective_id=0, has_side_effects=True, vmem_limit_bytes=24 << 20),
        name="gather",
    )(count, feat, adj, pos, *params)
    return out[0], out[1], out[2:]


def prepare(count, gf_ref, sum_ref, disp_ref, dist_ref, dd_ref, list_ref, pack_ref, tg_ref, gw_ref):
    gw_ref[0:8] = sum_ref[0:F, 0:F].T.reshape(8, WROWS, F)
    gw_ref[8] = sum_ref[0:F, F:F + 2 * NRBF].T[0:WROWS]
    rest = sum_ref[F:2 * F, F:F + 2 * NRBF].T
    gw_ref[9] = rest[NRBF:2 * NRBF]
    gw_ref[10] = rest[0:NRBF]
    gw_ref[12:16] = jnp.zeros((4, WROWS, F), f32)
    gw_ref[11] = jnp.full((WROWS, F), count, jnp.int32).astype(f32)
    pack_ref[:, 0:ATOMS, :] = gf_ref[...].reshape(BRICKS, ATOMS, F).astype(bf16)
    lists = list_ref[...]
    columns = lists.T.astype(jnp.int32)
    rows = lists[:, 0:ROWS].astype(jnp.int32)
    group = iota((ROWS, F), 1) >> 5
    in_u = group == (columns[0:ROWS, 0:1] & 3)
    in_v = group == (columns[0:ROWS, 1:2] & 3)
    rrow, srow = rows[0:1], rows[1:2]
    rep4 = (iota((F, PAIRS), 1) >> 5 == (iota((F, PAIRS), 0) & 31)).astype(bf16)
    til4 = ((iota((F, PAIRS), 1) & 31) == (iota((F, PAIRS), 0) & 31)).astype(bf16)
    radial = dd_ref[...] / dist_ref[...]
    t_sum = jnp.zeros((48, F), f32)
    p_sum = jnp.zeros((256, F), f32)
    to_u = (rrow >> 3) * 16 + ((rrow >> 2) & 1) * 3
    to_v = (srow >> 3) * 16 + ((srow >> 2) & 1) * 3
    pulls = jnp.concatenate([part for d in range(3) for part in split(disp_ref[d] * radial)], axis=0)
    recv_all = dot(pulls, rep4, NT)
    send_all = dot(pulls, til4, NT)
    for d in range(3):
        at = 2 * ROWS * d
        recv_hi, recv_lo = split(jnp.where(in_u, recv_all[at:at + ROWS] + recv_all[at + ROWS:at + 2 * ROWS], 0.0))
        send_hi, send_lo = split(jnp.where(in_v, send_all[at:at + ROWS] + send_all[at + ROWS:at + 2 * ROWS], 0.0))
        put_u = (to_u + d == iota((48, ROWS), 0)).astype(bf16)
        put_v = (to_v + d == iota((256, ROWS), 0)).astype(bf16)
        t_sum = t_sum + dot(put_u, recv_hi) + dot(put_u, recv_lo)
        p_sum = p_sum - dot(put_v, send_hi) - dot(put_v, send_lo)
    tg_ref[...] = t_sum.reshape(3, 16, F)
    pack_ref[:, ATOMS:PACK, :] = p_sum.astype(bf16).reshape(BRICKS, 16, F)


def reduce_kernel(
    cnt_s, gf_ref, sum_ref, disp_ref, dist_ref, dd_ref, list_ref, acc_ref, w3_buf,
    pack_ref, tg_ref, gw_ref, mate_buf, send_buf, chip_buf, tower_buf, w1_buf, w2_own, w2_buf,
    mate_send, mate_recv, chip_send, chip_recv, tower_send, tower_recv, w_send, w_recv,
):
    t = lax.axis_index("tower")
    p = lax.axis_index("plate")
    q, core = p // 2, p % 2
    mate = (t, q * 2 + 1 - core)
    chips = [(q + d) % 8 for d in range(8)]
    plate = [(t, (p + d) % 16) for d in range(16)]
    tower = [((t + d) % 16, p) for d in range(16)]
    barrier = pltpu.get_barrier_semaphore()
    peers = plate[1:] + tower[1:]
    for device in peers:
        pl.semaphore_signal(barrier, inc=1, device_id=device, device_id_type=pl.DeviceIdType.MESH)
    prepare(cnt_s[0, 0], gf_ref, sum_ref, disp_ref, dist_ref, dd_ref, list_ref, pack_ref, tg_ref, gw_ref)
    pl.semaphore_wait(barrier, len(peers))
    first = [send_to(gw_ref.at[(p + d) % 16], w1_buf.at[d], w_send.at[0], w_recv.at[0], d, plate[d]) for d in range(1, 16)]
    halves = [send_to(pack_ref.at[chips[d] * 2 + 1 - core], mate_buf.at[d], mate_send, mate_recv, d, mate) for d in (1, 2, 3, 4, 5, 6, 7, 0)]
    up = send_to(tg_ref.at[2], tower_buf.at[0], tower_send, tower_recv, 0, tower[1])
    down = send_to(tg_ref.at[0], tower_buf.at[1], tower_send, tower_recv, 1, tower[15])
    total = gw_ref[p]
    for d in range(1, 16):
        first[d - 1].wait_recv()
        total = total + w1_buf[d]
    w2_own[...] = total
    second = [send_to(w2_own, w2_buf.at[d], w_send.at[1], w_recv.at[1], d, tower[d]) for d in range(1, 16)]
    chip = []
    for d in range(1, 8):
        halves[d - 1].wait_recv()
        send_buf[d] = (pack_ref[chips[d] * 2 + core].astype(f32) + mate_buf[d].astype(f32)).astype(bf16)
        chip.append(send_to(send_buf.at[d], chip_buf.at[d], chip_send, chip_recv, d, (t, chips[d] * 2 + core)))
    for d in range(1, 16):
        second[d - 1].wait_recv()
        total = total + w2_buf[d]
    w3_buf[p] = total
    third = [send_to(w3_buf.at[p], w3_buf.at[p], w_send.at[2], w_recv.at[2], d, plate[d]) for d in range(1, 16)]
    halves[7].wait_recv()
    acc = pack_ref[p].astype(f32) + mate_buf[0].astype(f32)
    for d in range(1, 8):
        chip[d - 1].wait_recv()
        acc = acc + chip_buf[d].astype(f32)
    acc_ref[0:ATOMS, :] = acc[0:ATOMS]
    up.wait_recv()
    down.wait_recv()
    acc_ref[ATOMS:PACK, :] = acc[ATOMS:PACK] + tg_ref[1] + tower_buf[0] + tower_buf[1]
    for d in range(1, 16):
        third[d - 1].wait_recv()
    for copy in first + halves + [up, down] + second + chip + third:
        copy.wait_send()


def reduce(count, *partials):
    smem = pl.BlockSpec(memory_space=pltpu.SMEM)
    vmem = pl.BlockSpec(memory_space=pltpu.VMEM)
    weights = pltpu.VMEM((16, WROWS, F), f32)
    dma = pltpu.SemaphoreType.DMA
    return pl.pallas_call(
        reduce_kernel,
        out_shape=(jax.ShapeDtypeStruct((PACK, F), f32), jax.ShapeDtypeStruct((16, WROWS, F), f32)),
        in_specs=[smem] + [vmem] * 6,
        out_specs=[vmem] * 2,
        scratch_shapes=[pltpu.VMEM((BRICKS, PACK, F), bf16), pltpu.VMEM((3, 16, F), f32), weights] + [pltpu.VMEM((8, PACK, F), bf16)] * 3 + [
            pltpu.VMEM((2, 16, F), f32), weights, pltpu.VMEM((WROWS, F), f32), weights,
            dma((8,)), dma((8,)), dma((8,)), dma((8,)), dma((2,)), dma((2,)), dma((3, 16)), dma((3, 16)),
        ],
        compiler_params=pltpu.CompilerParams(collective_id=1, has_side_effects=True, vmem_limit_bytes=24 << 20),
        name="reduce",
    )(count, *partials)


def finish_kernel(cnt_s, acc_ref, w_ref, gf_out, gp_out, wr_out, br_out, wf_out, bf_out):
    gf_out[0] = jnp.where(iota((ATOMS, F), 0) < cnt_s[0, 0], acc_ref[0:ATOMS, :], 0.0)
    for k in range(2):
        for d in range(3):
            gp_out[d, :, k * F:(k + 1) * F] = acc_ref[ATOMS + 3 * k + d:ATOMS + 3 * k + d + 1, :]
    scale = lax.rsqrt(w_ref[11][0:1] * (TILE * TILE))
    wf_out[...] = w_ref[0:8].reshape(F, F) * -scale
    bf_out[...] = w_ref[8][0:1] * scale
    wr_out[...] = w_ref[9] * scale
    br_out[...] = w_ref[10][0:1] * scale


def finish(count, acc, weights):
    smem = pl.BlockSpec(memory_space=pltpu.SMEM)
    vmem = pl.BlockSpec(memory_space=pltpu.VMEM)
    return pl.pallas_call(
        finish_kernel,
        out_shape=(
            jax.ShapeDtypeStruct((1, ATOMS, F), f32), jax.ShapeDtypeStruct((3, 1, ATOMS), f32), jax.ShapeDtypeStruct((NRBF, F), f32),
            jax.ShapeDtypeStruct((1, F), f32), jax.ShapeDtypeStruct((F, F), f32), jax.ShapeDtypeStruct((1, F), f32),
        ),
        in_specs=[smem, vmem, vmem],
        out_specs=[vmem] * 6,
        compiler_params=pltpu.CompilerParams(vmem_limit_bytes=8 << 20),
        name="finish",
    )(count, acc, weights)


def local(features, adjoint, positions, w_rbf, b_rbf, w_filter, b_filter, atom_counts, tile_counts, tower_tiles, plate_tiles, image_shifts):
    params = [pltpu.with_memory_space_constraint(x, pltpu.HBM) for x in (tower_tiles, plate_tiles, image_shifts, w_rbf, b_rbf.reshape(1, F), w_filter, b_filter.reshape(1, F))]
    plate, tower, params = gather(atom_counts, *[pltpu.with_memory_space_constraint(x, pltpu.HBM) for x in (features[0], adjoint[0], positions[:, 0, :])], params)
    partials = pairs(tile_counts, tower, plate, params)
    gf, gp, wr, br, wf, bf = finish(atom_counts, *reduce(tile_counts, *partials))
    return gf, gp, wr, br[0], wf, bf[0]


def solution(mesh):
    from jax.sharding import PartitionSpec as P
    brick = P("tower", "plate", None)
    one = P("tower", "plate")
    return jax.shard_map(
        local, mesh=mesh,
        in_specs=(brick, brick, P(None, "tower", "plate"), P(), P(), P(), P(), one, one, brick, brick, brick),
        out_specs=(brick, P(None, "tower", "plate"), P(), P(), P(), P()),
        check_vma=False,
    )
```

```python
import math

import jax
import jax.numpy as jnp
from jax import lax
from jax.experimental import pallas as pl
from jax.experimental.pallas import tpu as pltpu

F = 128
TILE = 32
PAIRS = TILE * TILE
MAXT = 56
ATOMS = 256
PACK = ATOMS + 16
BRICKS = 16
WROWS = 16
ROWS = 64
TOWER = 24
PLATE = 128
NRBF = 16
cutoff = 3.0
soften = 0.01
sharp = 10.0
f32 = jnp.float32
bf16 = jnp.bfloat16

NN = (((1,), (0,)), ((), ()))
NT = (((1,), (1,)), ((), ()))
TN = (((0,), (0,)), ((), ()))


def dot(a, b, dims=NN):
    return lax.dot_general(a, b, dims, preferred_element_type=f32)


def iota(shape, axis):
    return lax.broadcasted_iota(jnp.int32, shape, axis)


def split(x):
    hi = x.astype(bf16)
    return hi, (x - hi.astype(f32)).astype(bf16)


def sine(x):
    y = x * x
    acc = jnp.full_like(x, 1.0 / 6227020800.0)
    for c in (-1.0 / 39916800.0, 1.0 / 362880.0, -1.0 / 5040.0, 1.0 / 120.0, -1.0 / 6.0, 1.0):
        acc = acc * y + c
    return acc * x


def three(x):
    hi = x.astype(bf16).astype(f32)
    mid = (x - hi).astype(bf16).astype(f32)
    return [hi, mid, x - hi - mid]


def pairs_kernel(
    cnt_s,
    tower_ref, plate_ref, u_ref, v_ref, c_ref,
    wr_ref, br_ref, wf_ref, bf_ref,
    gf_ref, sum_ref, disp_ref, dist_ref, dd_ref, list_ref,
    env_ref, tan_ref, rep_ref, u_s, v_s, flag_ref, flag_s, order_s, list_sem,
    *, chunk, tiles,
):
    count = cnt_s[0, 0]
    lists_in = [pltpu.make_async_copy(u_ref, u_s, list_sem.at[0]), pltpu.make_async_copy(v_ref, v_s, list_sem.at[1])]
    for copy in lists_in:
        copy.start()
    list_ref[...] = jnp.zeros(list_ref.shape, f32)
    for k, ref in enumerate((u_ref, v_ref, c_ref)):
        list_ref[k:k + 1, 0:MAXT] = ref[0].astype(f32)
    lists = list_ref[...]
    columns = lists.T.astype(jnp.int32)
    ucol = columns[0:ROWS, 0:1]
    vcol = columns[0:ROWS, 1:2]
    ccol = columns[0:ROWS, 2:3]
    rep = (iota((TILE, PAIRS), 1) >> 5 == iota((TILE, PAIRS), 0)).astype(bf16)
    rep_ref[...] = rep
    rep4 = (iota((F, PAIRS), 1) >> 5 == (iota((F, PAIRS), 0) & 31)).astype(bf16)
    til4 = ((iota((F, PAIRS), 1) & 31) == (iota((F, PAIRS), 0) & 31)).astype(bf16)
    group = iota((ROWS, F), 1) >> 5
    in_u = group == (ucol & 3)
    in_v = group == (vcol & 3)
    row_u = (ucol >> 3) * 16 + ((ucol >> 2) & 1) * 3
    row_v = (vcol >> 3) * 16 + ((vcol >> 2) & 1) * 3
    t_pos = tower_ref[:, ATOMS:PACK, :].reshape(48, F)
    p_pos = plate_ref[:, ATOMS:PACK, :].reshape(256, F)
    third = (ccol >= 3).astype(jnp.int32) + (ccol >= 6).astype(jnp.int32)
    shifts = (third - 1, ccol - 3 * third - 1, (ucol >> 3) - 1)
    pick_u = ((ucol >> 3) * 16 + 6 == iota((ROWS, 48), 1)).astype(bf16)
    pick_v = ((vcol >> 3) * 16 + 6 == iota((ROWS, 256), 1)).astype(bf16)
    first_u = ((ucol & 7) * TILE).astype(f32)
    first_v = ((vcol & 7) * TILE).astype(f32)
    live = (first_u < dot(pick_u, t_pos)) & (first_v < dot(pick_v, p_pos)) & (iota((ROWS, F), 0) < count)
    flag_ref[...] = live.astype(f32).T[0:8].astype(jnp.int32)
    flags = pltpu.make_async_copy(flag_ref, flag_s, list_sem.at[2])
    flags.start()
    square = jnp.zeros((ROWS, PAIRS), f32)
    for d in range(3):
        pick_u = (row_u + d == iota((ROWS, 48), 1)).astype(bf16)
        pick_v = (row_v + d == iota((ROWS, 256), 1)).astype(bf16)
        recv = jnp.where(in_u, dot(pick_u, t_pos), 0.0)
        send = jnp.where(in_v, dot(pick_v, p_pos), 0.0)
        disp = dot(recv.astype(bf16), rep4) - dot(send.astype(bf16), til4) + shifts[d].astype(f32)
        disp_ref[d] = disp
        square = square + disp * disp
    dist = jnp.sqrt(square + soften)
    dist_ref[...] = dist
    inside = (dist < cutoff) & (iota((ROWS, PAIRS), 0) < count)
    theta = jnp.minimum(dist, cutoff) * (math.pi / (2 * cutoff))
    cosine = jnp.maximum(sine(math.pi / 2 - theta), 1e-6)
    env_ref[...] = jnp.where(inside, cosine * cosine, 0.0)
    tan_ref[...] = jnp.where(inside, (-math.pi / cutoff) * sine(theta) / cosine, 0.0)
    dd_ref[...] = jnp.zeros((ROWS, PAIRS), f32)
    gf_ref[...] = jnp.zeros(gf_ref.shape, f32)
    sum_ref[...] = jnp.zeros(sum_ref.shape, f32)

    centres = iota((NRBF, 1), 0).astype(f32) * (cutoff / (NRBF - 1))
    ones = jnp.ones((NRBF, chunk), bf16)
    wr = wr_ref[...]
    zeros = jnp.zeros((NRBF - 3, F), f32)
    w1 = jnp.concatenate([wr.astype(f32) * 0.5] + three(br_ref[...] * 0.5) + [zeros], axis=0).T.astype(bf16)
    wf = wf_ref[...].astype(f32)
    nwft = jnp.concatenate([-wf.T, jnp.concatenate(three(bf_ref[...]) + [zeros], axis=0).T], axis=1).astype(bf16)
    hwf = (wf * 0.5).astype(bf16)
    fold = ((iota((TILE, 2 * F), 1) & 31) == iota((TILE, 2 * F), 0)).astype(bf16)

    def visit(entries, group):
        streams = []
        for e in entries:
            listed = jnp.minimum(e, MAXT - 1)
            u = u_s[0, 0, listed]
            v = v_s[0, 0, listed]
            adj = tower_ref[u >> 3, pl.ds(pl.multiple_of((u & 7) * TILE, TILE), TILE), :]
            adj = jnp.concatenate([adj] * 2, axis=0)
            feat = plate_ref[v >> 3, pl.ds(pl.multiple_of((v & 7) * TILE, TILE), TILE), :].astype(f32)
            feat4 = jnp.concatenate([feat] * 4, axis=0).T
            wide = jnp.concatenate([feat4] * (chunk // F), axis=1)
            for s in range(0, PAIRS, chunk):
                streams.append(dict(e=e, v=v, adj=adj, wide=wide, lanes=pl.ds(s, chunk)))

        def opening(x):
            x['off'] = dist_ref[pl.ds(x['e'], 1), x['lanes']] - centres
            x['basis'] = jnp.exp(-sharp * x['off'] * x['off'])
            x['inputs'] = jnp.concatenate([x['basis'].astype(bf16), ones], axis=0)
            x['half'] = dot(w1, x['inputs'])
            hi, lo = split(env_ref[pl.ds(x['e'], 1), x['lanes']])
            member = rep_ref[:, x['lanes']]
            spread = jnp.concatenate([member * hi, member * lo], axis=0)
            x['adj_env'] = dot(x['adj'], spread, TN)

        def middle(x):
            x['t'] = jnp.tanh(x['half'])
            x['soft_b'] = jnp.concatenate([jnp.log(1.0 - x['t']).astype(bf16), ones], axis=0)
            x['d_raw_b'] = (x['adj_env'] * x['wide']).astype(bf16)
            x['filt'] = dot(nwft, x['soft_b'])
            x['d_soft'] = dot(hwf, x['d_raw_b'])

        def closing(x):
            x['d_pre_b'] = (x['d_soft'] * (1.0 + x['t'])).astype(bf16)
            x['y'] = x['adj_env'] * x['filt']
            zsum = jnp.sum(x['y'] * x['wide'], axis=0, keepdims=True)
            d_basis = dot(wr, x['d_pre_b'])
            grads = jnp.concatenate([x['d_raw_b'], x['d_pre_b']], axis=0)
            values = jnp.concatenate([x['soft_b'], x['inputs'][0:NRBF]], axis=0)
            x['gw'] = dot(grads, values, NT)
            d_dist = jnp.sum(d_basis * x['basis'] * x['off'], axis=0, keepdims=True) * (-2.0 * sharp)
            x['dd'] = d_dist + tan_ref[pl.ds(x['e'], 1), x['lanes']] * zsum

        stages = (opening, middle, closing)
        groups = [streams[i:i + group] for i in range(0, len(streams), group)]
        for tick in range(len(groups) + len(stages) - 1):
            for lag, stage in enumerate(stages):
                if 0 <= tick - lag < len(groups):
                    for x in groups[tick - lag]:
                        stage(x)
        gw = streams[0]['gw']
        for x in streams[1:]:
            gw = gw + x['gw']
        for e in entries:
            acc = jnp.zeros((F, F), f32)
            for x in streams:
                if x['e'] is e:
                    v = x['v']
                    dd_ref[pl.ds(e, 1), x['lanes']] = x['dd']
                    for q in range(0, chunk, F):
                        acc = acc + x['y'][:, q:q + F]
            gf_ref[v] += dot(fold, jnp.concatenate(split(acc), axis=1), NT)
        sum_ref[...] += gw

    for copy in lists_in:
        copy.wait()
    flags.wait()

    def keep(e, n):
        order_s[n] = e
        return n + flag_s[0, e]

    kept = lax.fori_loop(0, MAXT, keep, 0)
    order_s[kept] = ROWS - 1
    whole = kept // tiles

    def many(step, carry):
        visit([order_s[step * tiles + k] for k in range(tiles)], 1024 // chunk)
        return carry

    def two(step, carry):
        visit([order_s[whole * tiles + 2 * step + k] for k in range(2)], 2 * PAIRS // chunk)
        return carry

    lax.fori_loop(0, whole, many, 0)
    lax.fori_loop(0, (kept - whole * tiles + 1) // 2, two, 0)


def pairs(count, tower, plate, params, chunk=256, tiles=7):
    smem = pl.BlockSpec(memory_space=pltpu.SMEM)
    vmem = pl.BlockSpec(memory_space=pltpu.VMEM)
    return pl.pallas_call(
        lambda *refs: pairs_kernel(*refs, chunk=chunk, tiles=tiles),
        out_shape=(
            jax.ShapeDtypeStruct((PLATE, TILE, F), f32),
            jax.ShapeDtypeStruct((2 * F, F + 2 * NRBF), f32),
            jax.ShapeDtypeStruct((3, ROWS, PAIRS), f32),
            jax.ShapeDtypeStruct((ROWS, PAIRS), f32),
            jax.ShapeDtypeStruct((ROWS, PAIRS), f32),
            jax.ShapeDtypeStruct((8, F), f32),
        ),
        in_specs=[smem] + [vmem] * 9,
        out_specs=[vmem] * 6,
        scratch_shapes=[
            pltpu.VMEM((ROWS, PAIRS), f32),
            pltpu.VMEM((ROWS, PAIRS), f32),
            pltpu.VMEM((TILE, PAIRS), bf16),
            pltpu.SMEM((1, 1, MAXT), jnp.int32),
            pltpu.SMEM((1, 1, MAXT), jnp.int32),
            pltpu.VMEM((8, ROWS), jnp.int32),
            pltpu.SMEM((8, ROWS), jnp.int32),
            pltpu.SMEM((ROWS,), jnp.int32),
            pltpu.SemaphoreType.DMA((3,)),
        ],
        compiler_params=pltpu.CompilerParams(vmem_limit_bytes=48 << 20),
        name="pairs",
    )(count, tower, plate, *params)


def send_to(src, dst, sends, recvs, slot, device):
    copy = pltpu.make_async_remote_copy(
        src_ref=src, dst_ref=dst, send_sem=sends.at[slot], recv_sem=recvs.at[slot],
        device_id=device, device_id_type=pl.DeviceIdType.MESH,
    )
    copy.start()
    return copy


def gather_kernel(
    cnt_s, feat_hbm, adj_hbm, pos_hbm, *refs,
):
    params_hbm, (plate_ref, tower_ref), params = refs[:7], refs[7:9], refs[9:16]
    feat_ref, adj_ref, pos_ref, local_sem, chip_send, chip_recv, mate_send, mate_recv, tower_send, tower_recv = refs[16:]
    t = lax.axis_index("tower")
    p = lax.axis_index("plate")
    q, core = p // 2, p % 2
    mate = (t, q * 2 + 1 - core)
    above = ((t + 1) % 16, p)
    below = ((t + 15) % 16, p)
    chips = [(q + d) % 8 for d in range(8)]
    back = [(q + 8 - d) % 8 for d in range(8)]
    local = []
    for k, (src, dst) in enumerate(zip((feat_hbm, adj_hbm, pos_hbm) + params_hbm, (feat_ref, adj_ref, pos_ref) + params)):
        local.append(pltpu.make_async_copy(src, dst, local_sem.at[k]))
        local[k].start()
    barrier = pltpu.get_barrier_semaphore()
    peers = [(t, chips[d] * 2 + core) for d in range(1, 8)] + [mate, above, below]
    for device in peers:
        pl.semaphore_signal(barrier, inc=1, device_id=device, device_id_type=pl.DeviceIdType.MESH)
    local[0].wait()
    local[1].wait()
    local[2].wait()
    live = iota((ATOMS, F), 0) < cnt_s[0, 0]
    halves = [pos_ref[:, k * F:(k + 1) * F].astype(f32) for k in range(2)]
    atoms = jnp.full((1, F), cnt_s[0, 0], jnp.int32).astype(f32)
    rows = jnp.concatenate(halves + [atoms, jnp.zeros((9, F), f32)], axis=0).astype(bf16)
    for src, ref, slot in ((feat_ref, plate_ref, p), (adj_ref, tower_ref, 1)):
        ref[slot, 0:ATOMS, :] = jnp.where(live, src[...].astype(f32), 0.0).astype(bf16)
        ref[slot, ATOMS:PACK, :] = rows
    pl.semaphore_wait(barrier, len(peers))
    mine = plate_ref.at[p]
    out = [send_to(mine, mine, chip_send, chip_recv, d, (t, chips[d] * 2 + core)) for d in range(1, 8)]
    out.append(send_to(mine, mine, mate_send, mate_recv, 0, mate))
    up = send_to(tower_ref.at[1], tower_ref.at[0], tower_send, tower_recv, 0, above)
    down = send_to(tower_ref.at[1], tower_ref.at[2], tower_send, tower_recv, 1, below)
    passed = []
    for d in range(1, 8):
        out[d - 1].wait_recv()
        block = plate_ref.at[back[d] * 2 + core]
        passed.append(send_to(block, block, mate_send, mate_recv, d, mate))
    for copy in local[3:]:
        copy.wait()
    for copy in out:
        copy.wait_send()
    out[7].wait_recv()
    for copy in passed + [up, down]:
        copy.wait()


def gather(count, feat, adj, pos, params):
    smem = pl.BlockSpec(memory_space=pltpu.SMEM)
    vmem = pl.BlockSpec(memory_space=pltpu.VMEM)
    hbm = pl.BlockSpec(memory_space=pltpu.HBM)
    out = pl.pallas_call(
        gather_kernel,
        out_shape=[jax.ShapeDtypeStruct((BRICKS, PACK, F), bf16), jax.ShapeDtypeStruct((3, PACK, F), bf16)]
        + [jax.ShapeDtypeStruct(x.shape, x.dtype) for x in params],
        in_specs=[smem] + [hbm] * 10,
        out_specs=[vmem] * 9,
        scratch_shapes=[pltpu.VMEM((ATOMS, F), bf16), pltpu.VMEM((ATOMS, F), bf16), pltpu.VMEM((3, ATOMS), bf16), pltpu.SemaphoreType.DMA((10,))]
        + [pltpu.SemaphoreType.DMA((8,))] * 4 + [pltpu.SemaphoreType.DMA((2,))] * 2,
        compiler_params=pltpu.CompilerParams(collective_id=0, has_side_effects=True, vmem_limit_bytes=24 << 20),
        name="gather",
    )(count, feat, adj, pos, *params)
    return out[0], out[1], out[2:]


def prepare(count, gf_ref, sum_ref, disp_ref, dist_ref, dd_ref, list_ref, pack_ref, tg_ref, gw_ref):
    gw_ref[0:8] = sum_ref[0:F, 0:F].T.reshape(8, WROWS, F)
    gw_ref[8] = sum_ref[0:F, F:F + 2 * NRBF].T[0:WROWS]
    rest = sum_ref[F:2 * F, F:F + 2 * NRBF].T
    gw_ref[9] = rest[NRBF:2 * NRBF]
    gw_ref[10] = rest[0:NRBF]
    gw_ref[12:16] = jnp.zeros((4, WROWS, F), f32)
    gw_ref[11] = jnp.full((WROWS, F), count, jnp.int32).astype(f32)
    pack_ref[:, 0:ATOMS, :] = gf_ref[...].reshape(BRICKS, ATOMS, F).astype(bf16)
    lists = list_ref[...]
    columns = lists.T.astype(jnp.int32)
    rows = lists[:, 0:ROWS].astype(jnp.int32)
    group = iota((ROWS, F), 1) >> 5
    in_u = group == (columns[0:ROWS, 0:1] & 3)
    in_v = group == (columns[0:ROWS, 1:2] & 3)
    rrow, srow = rows[0:1], rows[1:2]
    rep4 = (iota((F, PAIRS), 1) >> 5 == (iota((F, PAIRS), 0) & 31)).astype(bf16)
    til4 = ((iota((F, PAIRS), 1) & 31) == (iota((F, PAIRS), 0) & 31)).astype(bf16)
    radial = dd_ref[...] / dist_ref[...]
    t_sum = jnp.zeros((48, F), f32)
    p_sum = jnp.zeros((256, F), f32)
    to_u = (rrow >> 3) * 16 + ((rrow >> 2) & 1) * 3
    to_v = (srow >> 3) * 16 + ((srow >> 2) & 1) * 3
    pulls = jnp.concatenate([part for d in range(3) for part in split(disp_ref[d] * radial)], axis=0)
    recv_all = dot(pulls, rep4, NT)
    send_all = dot(pulls, til4, NT)
    for d in range(3):
        at = 2 * ROWS * d
        recv_hi, recv_lo = split(jnp.where(in_u, recv_all[at:at + ROWS] + recv_all[at + ROWS:at + 2 * ROWS], 0.0))
        send_hi, send_lo = split(jnp.where(in_v, send_all[at:at + ROWS] + send_all[at + ROWS:at + 2 * ROWS], 0.0))
        put_u = (to_u + d == iota((48, ROWS), 0)).astype(bf16)
        put_v = (to_v + d == iota((256, ROWS), 0)).astype(bf16)
        t_sum = t_sum + dot(put_u, recv_hi) + dot(put_u, recv_lo)
        p_sum = p_sum - dot(put_v, send_hi) - dot(put_v, send_lo)
    tg_ref[...] = t_sum.reshape(3, 16, F)
    pack_ref[:, ATOMS:PACK, :] = p_sum.astype(bf16).reshape(BRICKS, 16, F)


def reduce_kernel(
    cnt_s, gf_ref, sum_ref, disp_ref, dist_ref, dd_ref, list_ref, acc_ref, w3_buf,
    pack_ref, tg_ref, gw_ref, mate_buf, send_buf, chip_buf, tower_buf, w1_buf, w2_own, w2_buf,
    mate_send, mate_recv, chip_send, chip_recv, tower_send, tower_recv, w_send, w_recv,
):
    t = lax.axis_index("tower")
    p = lax.axis_index("plate")
    q, core = p // 2, p % 2
    mate = (t, q * 2 + 1 - core)
    chips = [(q + d) % 8 for d in range(8)]
    plate = [(t, (p + d) % 16) for d in range(16)]
    tower = [((t + d) % 16, p) for d in range(16)]
    barrier = pltpu.get_barrier_semaphore()
    peers = plate[1:] + tower[1:]
    for device in peers:
        pl.semaphore_signal(barrier, inc=1, device_id=device, device_id_type=pl.DeviceIdType.MESH)
    prepare(cnt_s[0, 0], gf_ref, sum_ref, disp_ref, dist_ref, dd_ref, list_ref, pack_ref, tg_ref, gw_ref)
    pl.semaphore_wait(barrier, len(peers))
    first = [send_to(gw_ref.at[(p + d) % 16], w1_buf.at[d], w_send.at[0], w_recv.at[0], d, plate[d]) for d in range(1, 16)]
    halves = [send_to(pack_ref.at[chips[d] * 2 + 1 - core], mate_buf.at[d], mate_send, mate_recv, d, mate) for d in (1, 2, 3, 4, 5, 6, 7, 0)]
    up = send_to(tg_ref.at[2], tower_buf.at[0], tower_send, tower_recv, 0, tower[1])
    down = send_to(tg_ref.at[0], tower_buf.at[1], tower_send, tower_recv, 1, tower[15])
    total = gw_ref[p]
    for d in range(1, 16):
        first[d - 1].wait_recv()
        total = total + w1_buf[d]
    w2_own[...] = total
    second = [send_to(w2_own, w2_buf.at[d], w_send.at[1], w_recv.at[1], d, tower[d]) for d in range(1, 16)]
    chip = []
    for d in range(1, 8):
        halves[d - 1].wait_recv()
        send_buf[d] = (pack_ref[chips[d] * 2 + core].astype(f32) + mate_buf[d].astype(f32)).astype(bf16)
        chip.append(send_to(send_buf.at[d], chip_buf.at[d], chip_send, chip_recv, d, (t, chips[d] * 2 + core)))
    for d in range(1, 16):
        second[d - 1].wait_recv()
        total = total + w2_buf[d]
    w3_buf[p] = total
    third = [send_to(w3_buf.at[p], w3_buf.at[p], w_send.at[2], w_recv.at[2], d, plate[d]) for d in range(1, 16)]
    halves[7].wait_recv()
    acc = pack_ref[p].astype(f32) + mate_buf[0].astype(f32)
    for d in range(1, 8):
        chip[d - 1].wait_recv()
        acc = acc + chip_buf[d].astype(f32)
    acc_ref[0:ATOMS, :] = acc[0:ATOMS]
    up.wait_recv()
    down.wait_recv()
    acc_ref[ATOMS:PACK, :] = acc[ATOMS:PACK] + tg_ref[1] + tower_buf[0] + tower_buf[1]
    for d in range(1, 16):
        third[d - 1].wait_recv()
    for copy in first + halves + [up, down] + second + chip + third:
        copy.wait_send()


def reduce(count, *partials):
    smem = pl.BlockSpec(memory_space=pltpu.SMEM)
    vmem = pl.BlockSpec(memory_space=pltpu.VMEM)
    weights = pltpu.VMEM((16, WROWS, F), f32)
    dma = pltpu.SemaphoreType.DMA
    return pl.pallas_call(
        reduce_kernel,
        out_shape=(jax.ShapeDtypeStruct((PACK, F), f32), jax.ShapeDtypeStruct((16, WROWS, F), f32)),
        in_specs=[smem] + [vmem] * 6,
        out_specs=[vmem] * 2,
        scratch_shapes=[pltpu.VMEM((BRICKS, PACK, F), bf16), pltpu.VMEM((3, 16, F), f32), weights] + [pltpu.VMEM((8, PACK, F), bf16)] * 3 + [
            pltpu.VMEM((2, 16, F), f32), weights, pltpu.VMEM((WROWS, F), f32), weights,
            dma((8,)), dma((8,)), dma((8,)), dma((8,)), dma((2,)), dma((2,)), dma((3, 16)), dma((3, 16)),
        ],
        compiler_params=pltpu.CompilerParams(collective_id=1, has_side_effects=True, vmem_limit_bytes=24 << 20),
        name="reduce",
    )(count, *partials)


def finish_kernel(cnt_s, acc_ref, w_ref, gf_out, gp_out, wr_out, br_out, wf_out, bf_out):
    gf_out[0] = jnp.where(iota((ATOMS, F), 0) < cnt_s[0, 0], acc_ref[0:ATOMS, :], 0.0)
    for k in range(2):
        for d in range(3):
            gp_out[d, :, k * F:(k + 1) * F] = acc_ref[ATOMS + 3 * k + d:ATOMS + 3 * k + d + 1, :]
    scale = lax.rsqrt(w_ref[11][0:1] * (TILE * TILE))
    wf_out[...] = w_ref[0:8].reshape(F, F) * -scale
    bf_out[...] = w_ref[8][0:1] * scale
    wr_out[...] = w_ref[9] * scale
    br_out[...] = w_ref[10][0:1] * scale


def finish(count, acc, weights):
    smem = pl.BlockSpec(memory_space=pltpu.SMEM)
    vmem = pl.BlockSpec(memory_space=pltpu.VMEM)
    return pl.pallas_call(
        finish_kernel,
        out_shape=(
            jax.ShapeDtypeStruct((1, ATOMS, F), f32), jax.ShapeDtypeStruct((3, 1, ATOMS), f32), jax.ShapeDtypeStruct((NRBF, F), f32),
            jax.ShapeDtypeStruct((1, F), f32), jax.ShapeDtypeStruct((F, F), f32), jax.ShapeDtypeStruct((1, F), f32),
        ),
        in_specs=[smem, vmem, vmem],
        out_specs=[vmem] * 6,
        compiler_params=pltpu.CompilerParams(vmem_limit_bytes=8 << 20),
        name="finish",
    )(count, acc, weights)


def local(features, adjoint, positions, w_rbf, b_rbf, w_filter, b_filter, atom_counts, tile_counts, tower_tiles, plate_tiles, image_shifts):
    params = [pltpu.with_memory_space_constraint(x, pltpu.HBM) for x in (tower_tiles, plate_tiles, image_shifts, w_rbf, b_rbf.reshape(1, F), w_filter, b_filter.reshape(1, F))]
    plate, tower, params = gather(atom_counts, *[pltpu.with_memory_space_constraint(x, pltpu.HBM) for x in (features[0], adjoint[0], positions[:, 0, :])], params)
    partials = pairs(tile_counts, tower, plate, params)
    gf, gp, wr, br, wf, bf = finish(atom_counts, *reduce(tile_counts, *partials))
    return gf, gp, wr, br[0], wf, bf[0]


def solution(mesh):
    from jax.sharding import PartitionSpec as P
    brick = P("tower", "plate", None)
    one = P("tower", "plate")
    return jax.shard_map(
        local, mesh=mesh,
        in_specs=(brick, brick, P(None, "tower", "plate"), P(), P(), P(), P(), one, one, brick, brick, brick),
        out_specs=(brick, P(None, "tower", "plate"), P(), P(), P(), P()),
        check_vma=False,
    )
```
